512 devices in a mesh: curve: 64 (over z, x, core), split: 8 (over y).
Axes of the slice: x: 4, y: 8, z: 8, core: 2. Of those that a mesh axis runs over, the one named last changes fastest.
Arguments:
- rhs_load: float32 [8192, 512], P(('curve', 'split')), may hold values from -6 to 6
- stretch: float32 [3, 8192], P(None, ('curve', 'split')), may hold values from 0.5 to 4
- helm_shift: float32 [8192], P(('curve', 'split')), may hold values from 100 to 1000
- local_slot: int32 [8192, 512], P(('curve', 'split')), may hold values from 0 to 5487, as said below
- share_curve: int32 [64, 8, 4, 128], P('curve', 'split'), may hold values from 0 to 5488, as said below
- share_split: int32 [64, 8, 2, 128], P('curve', 'split'), may hold values from 0 to 5488, as said below
- coarse_slot: int32 [8, 8192], P(None, ('curve', 'split')), may hold values from 0 to 15
- x_vals: float32 [16, 8192], P(None, ('curve', 'split')), may hold values from -4 to 4
- x_cols: int32 [16, 8192], P(None, ('curve', 'split')), may hold values from 0 to 8191, as said below
- x_count: int32 [8192], P(('curve', 'split')), may hold values from 1 to 16, as said below
Outputs:
- solution: float32 [8192, 512], P(('curve', 'split'))
- residual: float32 [8192, 512], P(('curve', 'split'))
The draws below stay inside these ranges and needn't reach their ends.
Inputs may be any that keep to these rules, and one draw needn't show every extreme that they name: `local_slot`: every slot 0 to 5487 of a device's node vector is named by one or more of its points. `share_curve`: each entry is a node slot of the device, or 5488 for an empty entry; the slots of one list are distinct; the list of device (c, s) for offset o and the partner's list for offset -o name shared nodes entry by entry and have equal numbers of filled entries, which come first; lists towards partitions that do not exist are empty; some list is full in every draw. `share_split`: as for share_curve, with partner (c, s + o) for the offsets -1 and 1. `x_cols`: entry 0 of row i is i; entries 1 to 7 lie within 32 of i; the later entries lie among the coarse unknowns of separator devices of a nested dissection of the device numbers, one level an entry. `x_count`: some rows use all 16 entries.
All inputs are finite; a program needn't handle non-finite values.
Results may differ from the reference program's by a relative error of at most 0.0009.
Values sent between devices are 32-bit elements; how exact they have to be, the bound alone decides.
No kernel may reach another device: no remote copies, remote signals or barrier semaphores. Data moves between devices by JAX's collectives and lax.ppermute only.
A program may use at most 64 MiB of HBM per device.

```python
import math
import jax
import jax.numpy as jnp
import numpy as np
from jax import lax

E_DEV = 16
POINTS = 512
ITERS = 4
REACH = 2
NNZ = 16
U_DEV = 5488
CAP = 128
CV_DEV = 16
NGROUP = 64
NLAYER = 8
ELEMS = 8192
NC = 8192


prime_steps = (999983, 1000003, 1000033, 1000037, 1000039)


def list_for_pair(pair_key, upper_side, partner_ok, forced_full):
    list_size = jax.random.randint(jax.random.fold_in(pair_key, 1), (), CAP // 2, CAP + 1)
    list_size = jnp.where(forced_full, CAP, list_size)
    role_key = jax.random.fold_in(pair_key, 2 + upper_side)
    first_slot = jax.random.randint(jax.random.fold_in(role_key, 3), (), 0, U_DEV)
    prime_pick = jax.random.randint(jax.random.fold_in(role_key, 4), (), 0, 5)
    stride = jnp.array(prime_steps, dtype=jnp.int32)[prime_pick] % U_DEV
    positions = jnp.arange(CAP, dtype=jnp.int32)
    slots_here = (first_slot + positions * stride) % U_DEV
    return jnp.where((positions < list_size) & partner_ok, slots_here, U_DEV).astype(jnp.int32)


def draw_share_curve(key, part):
    offsets = jnp.array(list(range(-REACH, 0)) + list(range(1, REACH + 1)), dtype=jnp.int32)
    group_ids, layer_ids, offset_ids = jnp.broadcast_arrays(jnp.arange(NGROUP, dtype=jnp.int32)[:, None, None], jnp.arange(NLAYER, dtype=jnp.int32)[None, :, None], offsets[None, None, :])
    partner = group_ids + offset_ids
    partner_ok = (partner >= 0) & (partner < NGROUP)
    lower_group = jnp.clip(jnp.minimum(group_ids, partner), 0, NGROUP - 1)
    distance = jnp.abs(offset_ids)
    upper_side = (offset_ids < 0).astype(jnp.int32)
    forced_full = (lower_group + layer_ids + distance) % 2 == 0

    def single_pair(lower_one, layer_one, distance_one, upper_one, ok_one, full_one):
        pair_key = jax.random.fold_in(jax.random.fold_in(jax.random.fold_in(jax.random.fold_in(key, 11), lower_one), layer_one), distance_one)
        return list_for_pair(pair_key, upper_one, ok_one, full_one)
    pair_lists = jax.vmap(single_pair)(lower_group.reshape(-1), layer_ids.reshape(-1), distance.reshape(-1), upper_side.reshape(-1), partner_ok.reshape(-1), forced_full.reshape(-1))
    return pair_lists.reshape(NGROUP, NLAYER, 2 * REACH, CAP)


def draw_share_split(key, part):
    offsets = jnp.array([-1, 1], dtype=jnp.int32)
    group_ids, layer_ids, offset_ids = jnp.broadcast_arrays(jnp.arange(NGROUP, dtype=jnp.int32)[:, None, None], jnp.arange(NLAYER, dtype=jnp.int32)[None, :, None], offsets[None, None, :])
    partner = layer_ids + offset_ids
    partner_ok = (partner >= 0) & (partner < NLAYER)
    lower_layer = jnp.clip(jnp.minimum(layer_ids, partner), 0, NLAYER - 1)
    upper_side = (offset_ids < 0).astype(jnp.int32)
    forced_full = (group_ids + lower_layer + 1) % 2 == 0

    def single_pair(group_one, lower_one, upper_one, ok_one, full_one):
        pair_key = jax.random.fold_in(jax.random.fold_in(jax.random.fold_in(key, 13), group_one), lower_one)
        return list_for_pair(pair_key, upper_one, ok_one, full_one)
    pair_lists = jax.vmap(single_pair)(group_ids.reshape(-1), lower_layer.reshape(-1), upper_side.reshape(-1), partner_ok.reshape(-1), forced_full.reshape(-1))
    return pair_lists.reshape(NGROUP, NLAYER, 2, CAP)


def draw_local_slot(key, part):
    device_keys = jax.random.split(jax.random.fold_in(key, 17), NGROUP * NLAYER)

    def single_device(device_key):
        repeats = jax.random.randint(jax.random.fold_in(device_key, 1), (E_DEV * POINTS - U_DEV,), 0, U_DEV)
        all_slots = jnp.concatenate([jnp.arange(U_DEV, dtype=jnp.int32), repeats.astype(jnp.int32)])
        return jax.random.permutation(jax.random.fold_in(device_key, 2), all_slots)
    return jax.vmap(single_device)(device_keys).reshape(ELEMS, POINTS).astype(jnp.int32)


def draw_x_cols(key, part):
    device_total = NGROUP * NLAYER
    level_total = max((device_total - 1).bit_length(), 1)
    row_ids = jnp.arange(NC, dtype=jnp.int32)[None, :]
    entry_ids = jnp.arange(NNZ, dtype=jnp.int32)[:, None]
    jitter = jax.random.randint(jax.random.fold_in(key, 19), (NNZ, NC), -2 * CV_DEV, 2 * CV_DEV + 1)
    near_columns = jnp.clip(row_ids + jitter, 0, NC - 1)
    level = level_total - 1 - jnp.maximum(entry_ids - NNZ // 2, 0) % level_total
    block = jnp.left_shift(jnp.ones_like(level), level + 1)
    row_device = row_ids // CV_DEV
    middle = row_device // block * block + block // 2
    middle = jnp.minimum(middle, device_total - 1)
    inside = jax.random.randint(jax.random.fold_in(key, 29), (NNZ, NC), 0, CV_DEV)
    separator_columns = middle * CV_DEV + inside
    columns = jnp.where(entry_ids >= NNZ // 2, separator_columns, near_columns)
    return jnp.where(entry_ids == 0, row_ids, columns).astype(jnp.int32)


def draw_x_count(key, part):
    counts_drawn = jax.random.randint(jax.random.fold_in(key, 23), (NC,), 1, NNZ + 1)
    full_rows = jnp.arange(NC) % 4 == 0
    return jnp.where(full_rows, NNZ, counts_drawn).astype(jnp.int32)


def with_ends(drawn, stream_key, low, high):
    longest = drawn.shape.index(max(drawn.shape))
    spots = []
    for shift in (0, 1):
        where = [jax.random.randint(jax.random.fold_in(stream_key, axis), (), 0, length) for axis, length in enumerate(drawn.shape)]
        where[longest] = (where[longest] + shift) % drawn.shape[longest]
        spots.append(tuple(where))
    return drawn.at[spots[0]].set(low).at[spots[1]].set(high)


def block_scale(own_key, shape, cuts, low, high):
    def one(axis_at, shards_of):
        steps = jax.random.uniform(jax.random.fold_in(jax.random.fold_in(own_key, 6), axis_at), (shards_of,), jnp.float32, low / len(cuts), high / len(cuts))
        return jnp.repeat(jnp.exp(steps), shape[axis_at] // shards_of).reshape((-1,) + (1,) * (len(shape) - axis_at - 1))

    factor_of = one(*cuts[0])
    for cut in cuts[1:]:
        factor_of = factor_of * one(*cut)
    return factor_of


def noise(rng, extent, width, most, pieces=(), held_as=jnp.bfloat16):
    values = width * jax.random.normal(rng, extent, jnp.float32)
    if pieces:
        values = values * block_scale(rng, extent, pieces, -0.22, 0.18)
    return jnp.clip(values, -most, most).astype(held_as)


def setup_inputs(seed: int = 0) -> dict:
    splits = jax.random.split(jax.random.key(seed), 11)
    return {
        "rhs_load": noise(splits[0], (ELEMS, POINTS), 1.0, 6.0, ((0, 512),), jnp.float32),
        "stretch": jnp.clip(jnp.exp(math.log(4.0) - 2.0794415 * jax.random.uniform(splits[1], (3, ELEMS), jnp.float32) ** block_scale(splits[1], (3, ELEMS), ((1, 512),), -0.2, 0.2)), 0.5, 4.0),
        "helm_shift": jnp.clip(jnp.exp(math.log(1000.0) - 2.3025851 * jax.random.uniform(splits[2], (ELEMS,), jnp.float32) ** block_scale(splits[2], (ELEMS,), ((0, 512),), -0.2, 0.2)), 100.0, 1000.0),
        "local_slot": draw_local_slot(jax.random.fold_in(splits[10], 71), 0),
        "share_curve": draw_share_curve(jax.random.fold_in(splits[10], 71), 0),
        "share_split": draw_share_split(jax.random.fold_in(splits[10], 71), 0),
        "coarse_slot": with_ends(jax.random.randint(splits[6], (8, ELEMS), 0, CV_DEV), jax.random.fold_in(splits[6], 1), 0, CV_DEV - 1).astype(jnp.int32),
        "x_vals": noise(splits[7], (NNZ, NC), 0.3, 4.0, ((1, 512),), jnp.float32),
        "x_cols": draw_x_cols(jax.random.fold_in(splits[10], 71), 0),
        "x_count": draw_x_count(jax.random.fold_in(splits[10], 71), 0),
    }


def element_tables():
    poly_order = 7
    node_count = poly_order + 1
    gll_nodes = -np.cos(np.pi * np.arange(node_count) / poly_order)
    legendre = np.zeros((node_count, node_count))
    for sweep in range(60):
        legendre[:, 0] = 1.0
        legendre[:, 1] = gll_nodes
        for degree in range(2, node_count):
            legendre[:, degree] = ((2 * degree - 1) * gll_nodes * legendre[:, degree - 1] - (degree - 1) * legendre[:, degree - 2]) / degree
        gll_nodes = gll_nodes - (gll_nodes * legendre[:, poly_order] - legendre[:, poly_order - 1]) / (node_count * legendre[:, poly_order])
    for degree in range(2, node_count):
        legendre[:, degree] = ((2 * degree - 1) * gll_nodes * legendre[:, degree - 1] - (degree - 1) * legendre[:, degree - 2]) / degree
    top_poly = legendre[:, poly_order]
    quad_weights = 2.0 / (poly_order * node_count * top_poly * top_poly)
    deriv_matrix = np.zeros((node_count, node_count))
    for row_index in range(node_count):
        for col_index in range(node_count):
            if row_index != col_index:
                deriv_matrix[row_index, col_index] = top_poly[row_index] / (top_poly[col_index] * (gll_nodes[row_index] - gll_nodes[col_index]))
    deriv_matrix[0, 0] = -poly_order * node_count / 4.0
    deriv_matrix[poly_order, poly_order] = poly_order * node_count / 4.0
    identity = np.eye(node_count)
    mass_diag = (quad_weights[:, None, None] * quad_weights[None, :, None] * quad_weights[None, None, :]).reshape(-1)
    stiff_list = []
    for deriv_kron in (np.kron(np.kron(deriv_matrix, identity), identity), np.kron(np.kron(identity, deriv_matrix), identity), np.kron(identity, np.kron(identity, deriv_matrix))):
        stiff_list.append(deriv_kron.T @ (mass_diag[:, None] * deriv_kron))
    stiffness = np.concatenate(stiff_list, axis=1)
    diag_index = np.arange(stiff_list[0].shape[0])
    stiff_diag = np.stack([block[diag_index, diag_index] for block in stiff_list])
    hat_values = np.stack([(1.0 - gll_nodes) / 2.0, (1.0 + gll_nodes) / 2.0])
    coarse_table = (hat_values[:, None, None, :, None, None] * hat_values[None, :, None, None, :, None] * hat_values[None, None, :, None, None, :]).reshape(8, -1)
    return mass_diag, stiffness, stiff_diag, coarse_table


def local_operator(element_field, stiffness, mass_diag, stretch, helm_shift):
    products = jnp.dot(element_field, stiffness, precision=lax.Precision.HIGHEST, preferred_element_type=jnp.float32)
    point_count = element_field.shape[1]
    result = stretch[0][:, None] * products[:, :point_count]
    result = result + stretch[1][:, None] * products[:, point_count:2 * point_count]
    result = result + stretch[2][:, None] * products[:, 2 * point_count:]
    return result + helm_shift[:, None] * mass_diag[None, :] * element_field


def node_sum(values, slot_row):
    return jax.ops.segment_sum(values, slot_row, num_segments=U_DEV + 1)


def add_at(base_row, values, slot_row):
    return base_row.at[slot_row].add(values)


def take_at(base_row, slot_row):
    return base_row[slot_row]


def assemble(fields, local_slot, share_curve, share_split):
    batch_count = fields.shape[0]
    per_device = fields.reshape(batch_count, NGROUP, NLAYER, E_DEV * POINTS)
    point_slots = local_slot.reshape(NGROUP, NLAYER, E_DEV * POINTS)
    summer = jax.vmap(jax.vmap(jax.vmap(node_sum)), in_axes=(0, None))
    adder = jax.vmap(jax.vmap(jax.vmap(add_at)), in_axes=(0, 0, None))
    taker = jax.vmap(jax.vmap(jax.vmap(take_at)), in_axes=(0, None))
    node_sums = summer(per_device, point_slots)
    assembled = node_sums
    reach = share_curve.shape[2] // 2
    curve_offsets = list(range(-reach, 0)) + list(range(1, reach + 1))
    group_ids = jnp.arange(NGROUP)
    for list_index, offset in enumerate(curve_offsets):
        outgoing = taker(node_sums, share_curve[:, :, 2 * reach - 1 - list_index, :])
        incoming = jnp.roll(outgoing, -offset, axis=1)
        partner = group_ids + offset
        partner_ok = (partner >= 0) & (partner < NGROUP)
        incoming = jnp.where(partner_ok[None, :, None, None], incoming, jnp.zeros_like(incoming))
        assembled = adder(assembled, incoming, share_curve[:, :, list_index, :])
    layer_ids = jnp.arange(NLAYER)
    for list_index, offset in enumerate((-1, 1)):
        outgoing = taker(node_sums, share_split[:, :, 1 - list_index, :])
        incoming = jnp.roll(outgoing, -offset, axis=2)
        partner = layer_ids + offset
        partner_ok = (partner >= 0) & (partner < NLAYER)
        incoming = jnp.where(partner_ok[None, None, :, None], incoming, jnp.zeros_like(incoming))
        assembled = adder(assembled, incoming, share_split[:, :, list_index, :])
    result = taker(assembled, point_slots)
    return result.reshape(batch_count, ELEMS, POINTS)


def reference(rhs_load, stretch, helm_shift, local_slot, share_curve, share_split, coarse_slot, x_vals, x_cols, x_count):
    mass_np, stiff_np, sdiag_np, coarse_np = element_tables()
    mass_diag = jnp.asarray(mass_np, dtype=jnp.float32)
    stiffness = jnp.asarray(stiff_np, dtype=jnp.float32)
    stiff_diag = jnp.asarray(sdiag_np, dtype=jnp.float32)
    coarse_table = jnp.asarray(coarse_np, dtype=jnp.float32)
    diag_local = stretch[0][:, None] * stiff_diag[0][None, :] + stretch[1][:, None] * stiff_diag[1][None, :]
    diag_local = diag_local + stretch[2][:, None] * stiff_diag[2][None, :] + helm_shift[:, None] * mass_diag[None, :]
    setup = assemble(jnp.stack([jnp.ones_like(rhs_load), diag_local, rhs_load]), local_slot, share_curve, share_split)
    multiplicity = setup[0]
    diag_a = setup[1]
    right = setup[2]
    owner = (jnp.arange(ELEMS) // E_DEV).astype(jnp.int32)
    coarse_ids = (coarse_slot + owner[None, :] * CV_DEV).astype(jnp.int32)
    live_entry = jnp.arange(NNZ)[:, None] < x_count[None, :]
    factor = jnp.where(live_entry, x_vals, jnp.zeros_like(x_vals))

    def inner(left_field, right_field):
        return jnp.sum(left_field * right_field / multiplicity)

    def precondition(residual_field):
        scaled = residual_field / multiplicity
        restricted = lax.dot_general(coarse_table, scaled, (((1,), (1,)), ((), ())), precision=lax.Precision.HIGHEST, preferred_element_type=jnp.float32)
        loads = jax.ops.segment_sum(restricted.reshape(-1), coarse_ids.reshape(-1), num_segments=NC)
        coarse_image = jax.ops.segment_sum((factor * loads[None, :]).reshape(-1), x_cols.reshape(-1), num_segments=NC)
        coarse_values = jnp.sum(factor * coarse_image[x_cols], axis=0)
        vertex_values = coarse_values[coarse_ids]
        correction = lax.dot_general(vertex_values, coarse_table, (((0,), (0,)), ((), ())), precision=lax.Precision.HIGHEST, preferred_element_type=jnp.float32)
        return residual_field / diag_a + correction

    def apply_operator(direction_field):
        return assemble(local_operator(direction_field, stiffness, mass_diag, stretch, helm_shift)[None], local_slot, share_curve, share_split)[0]

    solution = jnp.zeros_like(rhs_load)
    residual = right
    precond = precondition(residual)
    rz_value = inner(residual, precond)
    direction = precond
    for iteration in range(ITERS):
        image = apply_operator(direction)
        step_size = rz_value / inner(direction, image)
        solution = solution + step_size * direction
        residual = residual - step_size * image
        if iteration < ITERS - 1:
            precond = precondition(residual)
            rz_next = inner(residual, precond)
            direction = precond + (rz_next / rz_value) * direction
            rz_value = rz_next
    return solution, residual
```

```python
import functools

import jax
import jax.numpy as jnp
import ml_dtypes
import numpy as np
from jax import lax
from jax.experimental import pallas as pl
from jax.experimental.pallas import tpu as pltpu
from jax.sharding import PartitionSpec as P

ITERS = 4
HI = 48
LO = 128
ELEMS = 16
POINTS = 512
LISTS = 6
WIDE = ELEMS * POINTS
ENTRIES = 256
ROWS = 64
F32 = jnp.float32
BF16 = jnp.bfloat16
VMEM_LIMIT = 48 << 20


def element_tables():
    poly_order = 7
    node_count = poly_order + 1
    nodes = -np.cos(np.pi * np.arange(node_count) / poly_order)
    legendre = np.zeros((node_count, node_count))

    def fill():
        legendre[:, 0] = 1.0
        legendre[:, 1] = nodes
        for degree in range(2, node_count):
            legendre[:, degree] = (
                (2 * degree - 1) * nodes * legendre[:, degree - 1] - (degree - 1) * legendre[:, degree - 2]
            ) / degree

    for _ in range(60):
        fill()
        nodes = nodes - (nodes * legendre[:, poly_order] - legendre[:, poly_order - 1]) / (
            node_count * legendre[:, poly_order]
        )
    fill()
    top = legendre[:, poly_order]
    weights = 2.0 / (poly_order * node_count * top * top)
    deriv = np.zeros((node_count, node_count))
    for i in range(node_count):
        for j in range(node_count):
            if i != j:
                deriv[i, j] = top[i] / (top[j] * (nodes[i] - nodes[j]))
    deriv[0, 0] = -poly_order * node_count / 4.0
    deriv[poly_order, poly_order] = poly_order * node_count / 4.0
    mass = (weights[:, None, None] * weights[None, :, None] * weights[None, None, :]).reshape(-1)
    line = deriv.T @ (weights[:, None] * deriv)
    scaled = line / weights[None, :]
    eye = np.eye(node_count)
    first = np.kron(scaled, np.eye(64))
    second = np.kron(np.eye(4), np.kron(scaled, eye))
    third = np.kron(np.eye(4), np.kron(eye, scaled))
    diag = np.diag(scaled)
    ones = np.ones(node_count)
    diags = np.stack(
        [
            mass * np.kron(diag, np.kron(ones, ones)),
            mass * np.kron(ones, np.kron(diag, ones)),
            mass * np.kron(ones, np.kron(ones, diag)),
        ]
    )
    hats = np.stack([(1.0 - nodes) / 2.0, (1.0 + nodes) / 2.0])
    coarse = (
        hats[:, None, None, :, None, None]
        * hats[None, :, None, None, :, None]
        * hats[None, None, :, None, None, :]
    ).reshape(8, -1)
    return mass, first, np.concatenate([second, third], axis=1), diags, coarse


def halves(table):
    table = np.asarray(table, np.float32)
    upper = table.astype(ml_dtypes.bfloat16)
    lower = (table - upper.astype(np.float32)).astype(ml_dtypes.bfloat16)
    return upper, lower


def two_parts(value):
    upper = value.astype(BF16)
    return upper, (value - upper.astype(F32)).astype(BF16)


def row_mask(slots, height):
    high = lax.shift_right_logical(slots, 7)
    width = slots.shape[1]
    return jnp.broadcast_to(high, (height, width)) == lax.broadcasted_iota(jnp.int32, (height, width), 0)


def lane_hot(slots):
    low = lax.bitwise_and(slots, LO - 1)
    width = slots.shape[1]
    hot = jnp.broadcast_to(low, (LO, width)) == lax.broadcasted_iota(jnp.int32, (LO, width), 0)
    return jnp.where(hot, 1.0, 0.0).astype(BF16)


def spread(values, mask):
    parts = []
    for value in values:
        wide = jnp.where(mask, jnp.broadcast_to(value, mask.shape), 0.0)
        upper, lower = two_parts(wide)
        parts += [upper, lower]
    return jnp.concatenate(parts, axis=0)


def put(left, hot):
    return lax.dot_general(left, hot, (((1,), (1,)), ((), ())), preferred_element_type=F32)


def table_parts(table):
    upper, lower = two_parts(table)
    return jnp.concatenate([upper, lower], axis=1)


def take(parts, hot, mask):
    both = jnp.concatenate([hot, hot], axis=0)
    found = jnp.dot(parts, both, preferred_element_type=F32)
    return jnp.sum(jnp.where(mask, found, 0.0), axis=0, keepdims=True)


def fold(stacked, height):
    return stacked[:height] + stacked[height : 2 * height]


def total(value):
    return jnp.sum(jnp.sum(value, axis=1, keepdims=True), axis=0, keepdims=True)


def place(scalars):
    lane = lax.broadcasted_iota(jnp.int32, (1, LO), 1)
    row = jnp.zeros((1, LO), F32)
    for index, scalar in enumerate(scalars):
        row = jnp.where(lane == index, scalar, row)
    return row


def coarse_image(scaled, phi_ref, pick_ref, xcols, xhot):
    line = jnp.zeros((1, ENTRIES), F32)
    acc = jnp.zeros((ELEMS, ENTRIES), F32)
    for v in range(8):
        restricted = jnp.sum(scaled * phi_ref[v : v + 1, :], axis=1, keepdims=True)
        acc = acc + restricted * pick_ref[v]
    line = jnp.sum(acc, axis=0, keepdims=True)
    return fold(put(spread([line], row_mask(xcols, ROWS)), xhot), ROWS)


def coarse_correction(image, phi_ref, pick_ref, xcols, xhot):
    line = take(table_parts(image), xhot, row_mask(xcols, ROWS))
    result = jnp.zeros((ELEMS, POINTS), F32)
    for v in range(8):
        vertex = jnp.sum(pick_ref[v] * line, axis=1, keepdims=True)
        result = result + vertex * phi_ref[v : v + 1, :]
    return result


def write_payload(out_ref, image, scalars):
    row = place(scalars)
    for part in range(8):
        out_ref[part, 0:8, :] = image[8 * part : 8 * part + 8, :]
        out_ref[part, 8:9, :] = row


def setup_scatter(rhs_ref, slot_ref, list_ref, stretch_ref, helm_ref, mass_ref, diag_ref, hot_ref, sums_ref, *out_refs):
    diag = helm_ref[...] * mass_ref[...]
    for d in range(3):
        diag = diag + stretch_ref[:, d : d + 1] * diag_ref[d : d + 1, :]
    acc = jnp.zeros((6 * HI, LO), F32)
    for e in range(ELEMS):
        slots = slot_ref[e : e + 1, :]
        hot = lane_hot(slots)
        hot_ref[:, e * POINTS : (e + 1) * POINTS] = hot
        mask = row_mask(slots, HI)
        left = spread([jnp.ones((1, POINTS), F32), diag[e : e + 1, :], rhs_ref[e : e + 1, :]], mask)
        acc = acc + put(left, hot)
    tables = []
    for field in range(3):
        table = fold(acc[2 * HI * field : 2 * HI * (field + 1)], HI)
        sums_ref[field] = table
        tables.append(table_parts(table))
    for t in range(LISTS):
        slots = list_ref[t : t + 1, :]
        hot = lane_hot(slots)
        hot_ref[:, WIDE + t * LO : WIDE + (t + 1) * LO] = hot
        mask = row_mask(slots, HI)
        for field in range(3):
            out_refs[t][field : field + 1, :] = take(tables[field], hot, mask)


def incoming_table(list_ref, hot_ref, in_refs, field):
    acc = jnp.zeros((2 * HI, LO), F32)
    for t in range(LISTS):
        mask = row_mask(list_ref[t : t + 1, :], HI)
        left = spread([in_refs[t][field : field + 1, :]], mask)
        acc = acc + put(left, hot_ref[:, WIDE + t * LO : WIDE + (t + 1) * LO])
    return fold(acc, HI)


def setup_gather(
    slot_ref, list_ref, hot_ref, sums_ref, phi_ref, corner_ref, xvals_ref, xcols_ref, *refs
):
    in_refs = refs[:LISTS]
    minv_ref, dinv_ref, right_ref, pick_ref, xhot_ref, pay_ref = refs[LISTS:]
    tables = [
        table_parts(sums_ref[field] + incoming_table(list_ref, hot_ref, in_refs, field)) for field in range(3)
    ]
    for e in range(ELEMS):
        mask = row_mask(slot_ref[e : e + 1, :], HI)
        hot = hot_ref[:, e * POINTS : (e + 1) * POINTS]
        minv_ref[e : e + 1, :] = 1.0 / take(tables[0], hot, mask)
        dinv_ref[e : e + 1, :] = 1.0 / take(tables[1], hot, mask)
        right_ref[e : e + 1, :] = take(tables[2], hot, mask)
    xcols = xcols_ref[...]
    xhot_ref[...] = lane_hot(xcols)
    row_of = lax.bitwise_and(lax.broadcasted_iota(jnp.int32, (ELEMS, ENTRIES), 1), 15)
    for v in range(8):
        pick_ref[v] = jnp.where(corner_ref[:, v : v + 1] == row_of, xvals_ref[...], 0.0)
    scaled = right_ref[...] * minv_ref[...]
    image = coarse_image(scaled, phi_ref, pick_ref, xcols, xhot_ref[...])
    write_payload(pay_ref, image, [total(scaled * right_ref[...] * dinv_ref[...])])


def operator(u, stretch_ref, helm_ref, mass_ref, first_ref, second_ref):
    upper, lower = two_parts(u)

    def product(left_upper, left_lower, ref):
        rows = left_upper.shape[0]
        big = jnp.dot(
            jnp.concatenate([left_upper, left_lower], axis=0), ref[0], preferred_element_type=F32
        )
        return big[:rows] + big[rows:] + jnp.dot(left_upper, ref[1], preferred_element_type=F32)

    half = POINTS // 2
    along = product(upper, lower, first_ref)
    inside = product(
        jnp.concatenate([upper[:, :half], upper[:, half:]], axis=0),
        jnp.concatenate([lower[:, :half], lower[:, half:]], axis=0),
        second_ref,
    )
    second = jnp.concatenate([inside[:ELEMS, :half], inside[ELEMS:, :half]], axis=1)
    third = jnp.concatenate([inside[:ELEMS, half:], inside[ELEMS:, half:]], axis=1)
    result = stretch_ref[:, 0:1] * along + stretch_ref[:, 1:2] * second + stretch_ref[:, 2:3] * third
    return mass_ref[...] * (result + helm_ref[...] * u)


def apply_and_scatter(
    direction, slot_ref, list_ref, hot_ref, stretch_ref, helm_ref, mass_ref, first_ref, second_ref, field_ref, sums_ref, out_refs
):
    field_ref[...] = operator(direction, stretch_ref, helm_ref, mass_ref, first_ref, second_ref)
    acc = jnp.zeros((2 * HI, LO), F32)
    for e in range(ELEMS):
        mask = row_mask(slot_ref[e : e + 1, :], HI)
        left = spread([field_ref[e : e + 1, :]], mask)
        acc = acc + put(left, hot_ref[:, e * POINTS : (e + 1) * POINTS])
    table = fold(acc, HI)
    sums_ref[...] = table
    parts = table_parts(table)
    for t in range(LISTS):
        mask = row_mask(list_ref[t : t + 1, :], HI)
        out_refs[t][...] = take(parts, hot_ref[:, WIDE + t * LO : WIDE + (t + 1) * LO], mask)


def first_direction(
    slot_ref, list_ref, hot_ref, stretch_ref, helm_ref, mass_ref, first_ref, second_ref,
    phi_ref, pick_ref, xcols_ref, xhot_ref, dinv_ref, right_ref, pay_ref, *refs
):
    image_ref, state_ref, direction_ref, sums_ref = refs[:4]
    out_refs, field_ref = refs[4 : 4 + LISTS], refs[-1]
    for part in range(8):
        image_ref[8 * part : 8 * part + 8, :] = pay_ref[part, 0:8, :]
    image = image_ref[...]
    correction = coarse_correction(image, phi_ref, pick_ref, xcols_ref[...], xhot_ref[...])
    direction = right_ref[...] * dinv_ref[...] + correction
    direction_ref[...] = direction
    jacobi = pay_ref[0, 8:9, 0:1]
    state_ref[...] = place([jacobi, jacobi + total(image * image)])
    apply_and_scatter(
        direction, slot_ref, list_ref, hot_ref, stretch_ref, helm_ref, mass_ref, first_ref, second_ref, field_ref, sums_ref, out_refs
    )


def next_direction(
    slot_ref, list_ref, hot_ref, stretch_ref, helm_ref, mass_ref, first_ref, second_ref,
    phi_ref, pick_ref, xcols_ref, xhot_ref, dinv_ref, solution_ref, residual_ref, olddir_ref, force_ref,
    oldimage_ref, oldstate_ref, pay_ref, *refs
):
    newsol_ref, newres_ref, image_ref, state_ref, direction_ref, sums_ref = refs[:6]
    out_refs, field_ref = refs[6 : 6 + LISTS], refs[-1]
    jacobi = oldstate_ref[0:1, 0:1]
    rz_old = oldstate_ref[0:1, 1:2]
    alpha = rz_old / pay_ref[0, 8:9, 0:1]
    newsol_ref[...] = solution_ref[...] + alpha * olddir_ref[...]
    residual = residual_ref[...] - alpha * force_ref[...]
    newres_ref[...] = residual
    for part in range(8):
        rows = slice(8 * part, 8 * part + 8)
        image_ref[rows, :] = oldimage_ref[rows, :] - alpha * pay_ref[part, 0:8, :]
    image = image_ref[...]
    correction = coarse_correction(image, phi_ref, pick_ref, xcols_ref[...], xhot_ref[...])
    jacobi = jacobi - alpha * (2.0 * pay_ref[0, 8:9, 1:2] - alpha * pay_ref[0, 8:9, 2:3])
    rz_new = jacobi + total(image * image)
    direction = residual * dinv_ref[...] + correction + (rz_new / rz_old) * olddir_ref[...]
    direction_ref[...] = direction
    state_ref[...] = place([jacobi, rz_new])
    apply_and_scatter(
        direction, slot_ref, list_ref, hot_ref, stretch_ref, helm_ref, mass_ref, first_ref, second_ref, field_ref, sums_ref, out_refs
    )


def gather_image(slot_ref, list_ref, hot_ref, sums_ref, in_refs, force_ref):
    parts = table_parts(sums_ref[...] + incoming_table(list_ref, hot_ref, in_refs, 0))
    for e in range(ELEMS):
        mask = row_mask(slot_ref[e : e + 1, :], HI)
        force_ref[e : e + 1, :] = take(parts, hot_ref[:, e * POINTS : (e + 1) * POINTS], mask)


def assemble_reduce(
    slot_ref, list_ref, hot_ref, sums_ref, phi_ref, pick_ref, xcols_ref, xhot_ref, minv_ref, dinv_ref,
    residual_ref, direction_ref, *refs
):
    in_refs = refs[:LISTS]
    force_ref, pay_ref = refs[LISTS:]
    gather_image(slot_ref, list_ref, hot_ref, sums_ref, in_refs, force_ref)
    force = force_ref[...]
    scaled = force * minv_ref[...]
    smooth = scaled * dinv_ref[...]
    image = coarse_image(scaled, phi_ref, pick_ref, xcols_ref[...], xhot_ref[...])
    write_payload(
        pay_ref,
        image,
        [total(scaled * direction_ref[...]), total(smooth * residual_ref[...]), total(smooth * force)],
    )


def assemble_last(slot_ref, list_ref, hot_ref, sums_ref, minv_ref, direction_ref, *refs):
    in_refs = refs[:LISTS]
    force_ref, pay_ref = refs[LISTS:]
    gather_image(slot_ref, list_ref, hot_ref, sums_ref, in_refs, force_ref)
    pay_ref[...] = place([total(force_ref[...] * minv_ref[...] * direction_ref[...])])


def finish(solution_ref, residual_ref, direction_ref, force_ref, state_ref, pay_ref, newsol_ref, newres_ref):
    alpha = state_ref[0:1, 1:2] / jnp.sum(pay_ref[...], axis=0, keepdims=True)[:, 0:1]
    newsol_ref[...] = solution_ref[...] + alpha * direction_ref[...]
    newres_ref[...] = residual_ref[...] - alpha * force_ref[...]


def run(body, name, args, outs, scratch=()):
    return pl.pallas_call(
        body,
        name=name,
        out_shape=[jax.ShapeDtypeStruct(shape, dtype) for shape, dtype in outs],
        in_specs=[pl.BlockSpec(memory_space=pltpu.VMEM) for _ in args],
        out_specs=[pl.BlockSpec(memory_space=pltpu.VMEM) for _ in outs],
        scratch_shapes=list(scratch),
        compiler_params=pltpu.CompilerParams(vmem_limit_bytes=VMEM_LIMIT),
    )(*args)


def shift(block, axis, offset):
    size = lax.axis_size(axis)
    route = [(i, i + offset) for i in range(size) if 0 <= i + offset < size]
    return lax.ppermute(block, axis, route)


WAYS = (("split", -1), ("split", 1), ("curve", -2), ("curve", -1), ("curve", 1), ("curve", 2))


def exchange(outgoing):
    arrived = [None] * LISTS
    for t, (axis, offset) in enumerate(WAYS):
        back = WAYS.index((axis, -offset))
        arrived[back] = shift(outgoing[t], axis, offset)
    return arrived


def swap(block, axis):
    return lax.all_to_all(block, axis, 0, 0)


def reduce_all(payload):
    part = jnp.sum(swap(payload, "split"), axis=0)
    size = lax.axis_size("curve")
    part = jnp.sum(swap(jnp.broadcast_to(part[None], (size,) + part.shape), "curve"), axis=0)
    return swap(jnp.broadcast_to(part[None], payload.shape), "split")


def local(rhs_load, stretch, helm_shift, local_slot, share_curve, share_split, coarse_slot, x_vals, x_cols, x_count):
    mass, first, second, diags, coarse = element_tables()
    mass = jnp.asarray(mass.reshape(1, -1), F32)
    diags = jnp.asarray(diags, F32)
    phi = jnp.asarray(coarse, F32)
    first = jnp.asarray(np.stack(halves(first)))
    second = jnp.asarray(np.stack(halves(second)))
    stretch_t = stretch.T
    helm = helm_shift.reshape(-1, 1)
    corner = coarse_slot.T
    lists = jnp.concatenate([share_split.reshape(2, LO), share_curve.reshape(4, LO)], axis=0)
    factor = jnp.where(jnp.arange(x_vals.shape[0])[:, None] < x_count[None, :], x_vals, 0.0)
    xvals = factor.reshape(1, ENTRIES)
    xcols = x_cols.reshape(1, ENTRIES)
    field = ((ELEMS, POINTS), F32)
    table = ((HI, LO), F32)
    line = ((1, LO), F32)
    payload = ((8, 9, LO), F32)
    image_shape = ((ROWS, LO), F32)

    hot, sums3, *outgoing = run(
        setup_scatter,
        "setup_scatter",
        (rhs_load, local_slot, lists, stretch_t, helm, mass, diags),
        [((LO, WIDE + LISTS * LO), BF16), ((3, HI, LO), F32)] + [((3, LO), F32)] * LISTS,
    )
    arrived = exchange(outgoing)
    minv, dinv, right, pick, xhot, pay = run(
        setup_gather,
        "setup_gather",
        (local_slot, lists, hot, sums3, phi, corner, xvals, xcols, *arrived),
        [field, field, field, ((8, ELEMS, ENTRIES), F32), ((LO, ENTRIES), BF16), payload],
    )
    pay = reduce_all(pay)
    shape = (local_slot, lists, hot)
    elements = (stretch_t, helm, mass, first, second)
    grid = (phi, pick, xcols, xhot)
    scratch = [pltpu.VMEM((ELEMS, POINTS), F32)]
    solution = jnp.zeros_like(rhs_load)
    residual = right
    image, state, direction, sums, *outgoing = run(
        first_direction,
        "first_direction",
        (*shape, *elements, *grid, dinv, right, pay),
        [image_shape, line, field, table] + [line] * LISTS,
        scratch,
    )
    for iteration in range(ITERS):
        arrived = exchange(outgoing)
        if iteration < ITERS - 1:
            force, pay = run(
                assemble_reduce,
                "assemble_reduce",
                (*shape, sums, *grid, minv, dinv, residual, direction, *arrived),
                [field, payload],
            )
            pay = reduce_all(pay)
            solution, residual, image, state, direction, sums, *outgoing = run(
                next_direction,
                "next_direction",
                (*shape, *elements, *grid, dinv, solution, residual, direction, force, image, state, pay),
                [field, field, image_shape, line, field, table] + [line] * LISTS,
                scratch,
            )
        else:
            force, pay = run(
                assemble_last,
                "assemble_last",
                (*shape, sums, minv, direction, *arrived),
                [field, line],
            )
            devices = lax.axis_size("curve") * lax.axis_size("split")
            pay = lax.all_to_all(jnp.broadcast_to(pay[None], (devices, 1, LO)), ("curve", "split"), 0, 0)
            solution, residual = run(
                finish,
                "finish",
                (solution, residual, direction, force, state, pay.reshape(devices, LO)),
                [field, field],
            )
    return solution, residual


def solution(mesh):
    in_specs = (
        P(("curve", "split"), None),
        P(None, ("curve", "split")),
        P(("curve", "split")),
        P(("curve", "split"), None),
        P("curve", "split", None, None),
        P("curve", "split", None, None),
        P(None, ("curve", "split")),
        P(None, ("curve", "split")),
        P(None, ("curve", "split")),
        P(("curve", "split")),
    )
    out_specs = (P(("curve", "split"), None), P(("curve", "split"), None))
    return jax.shard_map(local, mesh=mesh, in_specs=in_specs, out_specs=out_specs, check_vma=False)
```

```python
import functools

import jax
import jax.numpy as jnp
import ml_dtypes
import numpy as np
from jax import lax
from jax.experimental import pallas as pl
from jax.experimental.pallas import tpu as pltpu
from jax.sharding import PartitionSpec as P

ITERS = 4
HI = 48
LO = 128
ELEMS = 16
POINTS = 512
LISTS = 6
WIDE = ELEMS * POINTS
ENTRIES = 256
ROWS = 64
CHUNK = 1024
F32 = jnp.float32
BF16 = jnp.bfloat16
VMEM_LIMIT = 16 << 20


def element_tables():
    poly_order = 7
    node_count = poly_order + 1
    nodes = -np.cos(np.pi * np.arange(node_count) / poly_order)
    legendre = np.zeros((node_count, node_count))

    def fill():
        legendre[:, 0] = 1.0
        legendre[:, 1] = nodes
        for degree in range(2, node_count):
            legendre[:, degree] = (
                (2 * degree - 1) * nodes * legendre[:, degree - 1] - (degree - 1) * legendre[:, degree - 2]
            ) / degree

    for _ in range(60):
        fill()
        nodes = nodes - (nodes * legendre[:, poly_order] - legendre[:, poly_order - 1]) / (
            node_count * legendre[:, poly_order]
        )
    fill()
    top = legendre[:, poly_order]
    weights = 2.0 / (poly_order * node_count * top * top)
    deriv = np.zeros((node_count, node_count))
    for i in range(node_count):
        for j in range(node_count):
            if i != j:
                deriv[i, j] = top[i] / (top[j] * (nodes[i] - nodes[j]))
    deriv[0, 0] = -poly_order * node_count / 4.0
    deriv[poly_order, poly_order] = poly_order * node_count / 4.0
    mass = (weights[:, None, None] * weights[None, :, None] * weights[None, None, :]).reshape(-1)
    line = deriv.T @ (weights[:, None] * deriv)
    scaled = line / weights[None, :]
    eye = np.eye(node_count)
    first = np.kron(scaled, np.eye(64))
    second = np.kron(np.eye(4), np.kron(scaled, eye))
    third = np.kron(np.eye(4), np.kron(eye, scaled))
    diag = np.diag(scaled)
    ones = np.ones(node_count)
    diags = np.stack(
        [
            mass * np.kron(diag, np.kron(ones, ones)),
            mass * np.kron(ones, np.kron(diag, ones)),
            mass * np.kron(ones, np.kron(ones, diag)),
        ]
    )
    hats = np.stack([(1.0 - nodes) / 2.0, (1.0 + nodes) / 2.0])
    coarse = (
        hats[:, None, None, :, None, None]
        * hats[None, :, None, None, :, None]
        * hats[None, None, :, None, None, :]
    ).reshape(8, -1)
    return mass, first, np.concatenate([second, third], axis=1), diags, coarse


def table_pieces(table):
    rest = np.asarray(table, np.float32)
    pieces = []
    for _ in range(3):
        piece = rest.astype(ml_dtypes.bfloat16)
        pieces.append(piece)
        rest = rest - piece.astype(np.float32)
    return np.stack(pieces)


def pieces(value):
    upper = value.astype(BF16)
    rest = value - upper.astype(F32)
    middle = rest.astype(BF16)
    return [upper, middle, (rest - middle.astype(F32)).astype(BF16)]


def row_mask(slots, height):
    high = lax.shift_right_logical(slots, 7)
    width = slots.shape[1]
    return jnp.broadcast_to(high, (height, width)) == lax.broadcasted_iota(jnp.int32, (height, width), 0)


def lane_hot(slots):
    low = lax.bitwise_and(slots, LO - 1)
    width = slots.shape[1]
    hot = jnp.broadcast_to(low, (LO, width)) == lax.broadcasted_iota(jnp.int32, (LO, width), 0)
    return jnp.where(hot, 1.0, 0.0).astype(BF16)


def spread(values, mask):
    wide = [jnp.where(mask, jnp.broadcast_to(value, mask.shape), 0.0) for value in values]
    return jnp.concatenate([piece for value in wide for piece in pieces(value)], axis=0)


def put(left, hot):
    return lax.dot_general(left, hot, (((1,), (1,)), ((), ())), preferred_element_type=F32)


def table_parts(table):
    return jnp.concatenate(pieces(table), axis=1)


def take(parts, hot, mask):
    found = jnp.dot(parts, jnp.concatenate([hot] * 3, axis=0), preferred_element_type=F32)
    return jnp.sum(jnp.where(mask, found, 0.0), axis=0, keepdims=True)


def fold(stacked, height):
    return stacked[:height] + stacked[height : 2 * height] + stacked[2 * height : 3 * height]


def total(value):
    return jnp.sum(jnp.sum(value, axis=1, keepdims=True), axis=0, keepdims=True)


def place(scalars):
    lane = lax.broadcasted_iota(jnp.int32, (1, LO), 1)
    row = jnp.zeros((1, LO), F32)
    for index, scalar in enumerate(scalars):
        row = jnp.where(lane == index, scalar, row)
    return row


def column(row):
    size = row.shape[1]
    square = lax.broadcasted_iota(jnp.int32, (size, size), 0) == lax.broadcasted_iota(jnp.int32, (size, size), 1)
    return jnp.sum(jnp.where(square, jnp.broadcast_to(row, (size, size)), 0.0), axis=1, keepdims=True)


def flatten(square):
    lane = lax.broadcasted_iota(jnp.int32, (16, ENTRIES), 1)
    sub = lax.broadcasted_iota(jnp.int32, (16, ENTRIES), 0)
    spreader = jnp.where(lax.bitwise_and(lane, 15) == sub, 1.0, 0.0)
    wide = jnp.dot(square, spreader, precision=lax.Precision.HIGHEST, preferred_element_type=F32)
    return jnp.sum(jnp.where(lax.shift_right_logical(lane, 4) == sub, wide, 0.0), axis=0, keepdims=True)


def list_row(split_ref, curve_ref, t):
    return split_ref[0, 0, t : t + 1, :] if t < 2 else curve_ref[0, 0, t - 2 : t - 1, :]


def list_hot(hot_ref, t):
    return hot_ref[:, WIDE + t * LO : WIDE + (t + 1) * LO]


def point_hot(hot_ref, e):
    return hot_ref[:, e * POINTS : (e + 1) * POINTS]


def owner_mask():
    lane = lax.broadcasted_iota(jnp.int32, (ELEMS, ENTRIES), 1)
    return lax.bitwise_and(lane, 15) == lax.broadcasted_iota(jnp.int32, (ELEMS, ENTRIES), 0)


def coarse_line(scaled, phi_ref, pick_ref):
    acc = jnp.zeros((ELEMS, ENTRIES), F32)
    for v in range(8):
        restricted = jnp.sum(scaled * phi_ref[v : v + 1, :], axis=1, keepdims=True)
        acc = acc + restricted * pick_ref[v]
    return jnp.sum(acc, axis=0, keepdims=True)


def coarse_correction(image, phi_ref, pick_ref, xcols, xhot):
    line = take(table_parts(image), xhot, row_mask(xcols, ROWS))
    result = jnp.zeros((ELEMS, POINTS), F32)
    for v in range(8):
        vertex = jnp.sum(pick_ref[v] * line, axis=1, keepdims=True)
        result = result + vertex * phi_ref[v : v + 1, :]
    return result


def image_of(line, cols, hot):
    return fold(put(spread([line], row_mask(cols, ROWS)), hot), ROWS)


def write_payload(pay_ref, image, rows):
    here = lax.axis_index("split")
    for g in range(8):
        for r in range(8):
            pay_ref[g, 0:1, r * LO : (r + 1) * LO] = image[8 * g + r : 8 * g + r + 1, :]
        row = jnp.where(here == g + 1, rows[0], jnp.where(here == g - 1, rows[1], jnp.zeros((1, LO), F32)))
        pay_ref[g, 0:1, CHUNK:] = row


def setup_scatter(
    rhs_ref, slot_ref, split_ref, curve_ref, stretch_ref, helm_ref, corner_ref, xvals_ref, xcols_ref, xcount_ref,
    mass_ref, diag_ref, phi_ref,
    hot_ref, sums_ref, scale_ref, line_ref, entry_ref, pick_ref, xhot_ref, *out_refs
):
    columns = [column(stretch_ref[d : d + 1, :]) for d in range(3)] + [column(helm_ref[...])]
    scale_ref[...] = jnp.concatenate(columns + columns, axis=1)
    diag = columns[3] * mass_ref[...]
    for d in range(3):
        diag = diag + columns[d] * diag_ref[d : d + 1, :]
    live = lax.broadcasted_iota(jnp.int32, (16, 16), 0) < jnp.broadcast_to(xcount_ref[...], (16, 16))
    factor = flatten(jnp.where(live, xvals_ref[...], 0.0))
    cols = flatten(xcols_ref[...].astype(F32))
    line_ref[...] = factor
    entries = (cols + 0.5).astype(jnp.int32)
    entry_ref[...] = entries
    xhot_ref[...] = lane_hot(entries)
    owner = lax.bitwise_and(lax.broadcasted_iota(jnp.int32, (ELEMS, ENTRIES), 1), 15)
    corners = [column(corner_ref[v : v + 1, :].astype(F32)) for v in range(8)]
    for v in range(8):
        pick_ref[v] = jnp.where((corners[v] + 0.5).astype(jnp.int32) == owner, factor, 0.0)
    corner = jnp.concatenate(corners, axis=1)
    lists = jnp.concatenate(
        [column(list_row(split_ref, curve_ref, t).astype(F32)) for t in range(LISTS)], axis=0
    )
    lists = (lists + 0.5).astype(jnp.int32)
    acc = jnp.zeros((9 * HI, LO), F32)
    weights = jnp.zeros((3 * ELEMS, LISTS * LO), F32)
    for e in range(ELEMS):
        slots = slot_ref[e : e + 1, :]
        hot = lane_hot(slots)
        hot_ref[:, e * POINTS : (e + 1) * POINTS] = hot
        mask = row_mask(slots, HI)
        left = spread([jnp.ones((1, POINTS), F32), diag[e : e + 1, :], rhs_ref[e : e + 1, :]], mask)
        acc = acc + put(left, hot)
        unknown = lax.broadcasted_iota(jnp.int32, (ELEMS, 8), 0).astype(F32)
        vertex = jnp.where(jnp.abs(corner[e : e + 1, :] - unknown) < 0.5, 1.0, 0.0)
        basis = jnp.dot(vertex, phi_ref[...], precision=lax.Precision.HIGHEST, preferred_element_type=F32)
        shape = (LISTS * LO, POINTS)
        same = jnp.where(jnp.broadcast_to(slots, shape) == jnp.broadcast_to(lists, shape), 1.0, 0.0)
        weights = weights + put(jnp.concatenate(pieces(basis), axis=0), same.astype(BF16))
    weights = fold(weights, ELEMS)
    tables = []
    for field in range(3):
        table = fold(acc[3 * HI * field : 3 * HI * (field + 1)], HI)
        sums_ref[field] = table
        tables.append(table_parts(table))
    for t in range(LISTS):
        slots = list_row(split_ref, curve_ref, t)
        hot = lane_hot(slots)
        hot_ref[:, WIDE + t * LO : WIDE + (t + 1) * LO] = hot
        mask = row_mask(slots, HI)
        rows = [take(tables[field], hot, mask) for field in range(3)]
        rows += [cols[:, :LO], cols[:, LO:], factor[:, :LO], factor[:, LO:], jnp.zeros((1, LO), F32)]
        for r in range(8):
            out_refs[t][r : r + 1, :] = rows[r]
        out_refs[t][8:24, :] = weights[:, t * LO : (t + 1) * LO]


def incoming_table(split_ref, curve_ref, hot_ref, rows):
    acc = jnp.zeros((3 * HI, LO), F32)
    for t in range(LISTS):
        mask = row_mask(list_row(split_ref, curve_ref, t), HI)
        acc = acc + put(spread([rows[t]], mask), list_hot(hot_ref, t))
    return fold(acc, HI)


def setup_gather(slot_ref, split_ref, curve_ref, hot_ref, sums_ref, phi_ref, pick_ref, entry_ref, xhot_ref, *refs):
    in_refs = refs[:LISTS]
    minv_ref, dinv_ref, right_ref, nline_ref, nentry_ref, nhot_ref, pay_ref, rows_ref = refs[LISTS:]
    tables = [
        table_parts(
            sums_ref[field] + incoming_table(split_ref, curve_ref, hot_ref, [ref[field : field + 1, :] for ref in in_refs])
        )
        for field in range(3)
    ]
    for e in range(ELEMS):
        mask = row_mask(slot_ref[e : e + 1, :], HI)
        hot = point_hot(hot_ref, e)
        minv_ref[e : e + 1, :] = 1.0 / take(tables[0], hot, mask)
        dinv_ref[e : e + 1, :] = 1.0 / take(tables[1], hot, mask)
        right_ref[e : e + 1, :] = take(tables[2], hot, mask)
    rows = []
    for t in range(LISTS):
        mult = take(tables[0], list_hot(hot_ref, t), row_mask(list_row(split_ref, curve_ref, t), HI))
        rows.append(jnp.where(mult > 0.5, 1.0 / jnp.where(mult > 0.5, mult, 1.0), 0.0))
        there = jnp.concatenate([in_refs[t][3:4, :], in_refs[t][4:5, :]], axis=1)
        entries = (there + 0.5).astype(jnp.int32)
        nentry_ref[t : t + 1, :] = entries
        nhot_ref[:, t * ENTRIES : (t + 1) * ENTRIES] = lane_hot(entries)
        nline_ref[t : t + 1, :] = jnp.concatenate([in_refs[t][5:6, :], in_refs[t][6:7, :]], axis=1)
    for t in range(2, LISTS):
        rows_ref[t - 2 : t - 1, :] = rows[t]
    line = coarse_line(right_ref[...] * minv_ref[...], phi_ref, pick_ref)
    write_payload(pay_ref, image_of(line, entry_ref[...], xhot_ref[...]), rows)


def operator(u, scale_ref, mass_ref, first_ref, second_ref):
    def product(parts, ref):
        rows = parts[0].shape[0]
        one = jnp.dot(jnp.concatenate(parts, axis=0), ref[0], preferred_element_type=F32)
        two = jnp.dot(jnp.concatenate(parts[:2], axis=0), ref[1], preferred_element_type=F32)
        three = jnp.dot(parts[0], ref[2], preferred_element_type=F32)
        return one[:rows] + (one[rows : 2 * rows] + two[:rows] + (one[2 * rows :] + two[rows:] + three))

    half = POINTS // 2
    parts = pieces(u)
    along = product(parts, first_ref)
    inside = product([jnp.concatenate([p[:, :half], p[:, half:]], axis=0) for p in parts], second_ref)
    second = jnp.concatenate([inside[:ELEMS, :half], inside[ELEMS:, :half]], axis=1)
    third = jnp.concatenate([inside[:ELEMS, half:], inside[ELEMS:, half:]], axis=1)
    result = scale_ref[:, 0:1] * along + scale_ref[:, 1:2] * second + scale_ref[:, 2:3] * third
    return mass_ref[...] * (result + scale_ref[:, 3:4] * u)


def scatter_points(field_ref, slot_ref, hot_ref):
    acc = jnp.zeros((3 * HI, LO), F32)
    for e in range(ELEMS):
        left = spread([field_ref[e : e + 1, :]], row_mask(slot_ref[e : e + 1, :], HI))
        acc = acc + put(left, point_hot(hot_ref, e))
    return fold(acc, HI)


def gather_points(table, slot_ref, hot_ref, out_ref):
    parts = table_parts(table)
    for e in range(ELEMS):
        out_ref[e : e + 1, :] = take(parts, point_hot(hot_ref, e), row_mask(slot_ref[e : e + 1, :], HI))


def send_lists(table, split_ref, curve_ref, hot_ref):
    parts = table_parts(table)
    return [
        take(parts, list_hot(hot_ref, t), row_mask(list_row(split_ref, curve_ref, t), HI)) for t in range(LISTS)
    ]


def halo_rows(shalo_ref, chalo_ref):
    return [shalo_ref[t : t + 1, :] for t in range(2)] + [chalo_ref[t : t + 1, :] for t in range(4)]


def krylov_step(index, last, *refs):
    (slot_ref, split_ref, curve_ref, hot_ref, scale_ref, mass_ref, first_ref, second_ref, phi_ref, pick_ref,
     entry_ref, xhot_ref, nline_ref, nentry_ref, nhot_ref, minv_ref, dinv_ref, norm_ref, gathered_ref,
     shalo_ref, chalo_ref) = refs[:21]
    refs = refs[21:]
    image_ref, field_ref = refs[-2:]
    refs = refs[:-2]
    rows = halo_rows(shalo_ref, chalo_ref)
    if index == 0:
        right_ref, *sent_refs = refs[:7]
        refs = refs[7:]
        force = right_ref[...]
    else:
        weight_ref, sums_ref = refs[:2]
        refs = refs[2:]
    base_ref, newnorm_ref, newsums_ref = refs[:3]
    refs = refs[3:]
    if index == 0:
        newweight_ref = refs[0]
        refs = refs[1:]
        for t in range(LISTS):
            newweight_ref[t] = sent_refs[t][8:24, :] * rows[t]
        weight_ref = newweight_ref
    else:
        force_ref = refs[0]
        refs = refs[1:]
        gather_points(
            sums_ref[...] + incoming_table(split_ref, curve_ref, hot_ref, rows), slot_ref, hot_ref, force_ref
        )
        force = force_ref[...]
    for g in range(8):
        for r in range(8):
            image_ref[8 * g + r : 8 * g + r + 1, :] = gathered_ref[g, 0:1, r * LO : (r + 1) * LO]
    image = image_ref[...]
    size = 1.0 + jnp.sqrt(total(image * image))
    lane = lax.broadcasted_iota(jnp.int32, (1, LO), 1)
    newnorm_ref[...] = jnp.where(lane == index, size, norm_ref[...]) if index else jnp.broadcast_to(size, (1, LO))
    correction = coarse_correction(image, phi_ref, pick_ref, entry_ref[...], xhot_ref[...])
    base = (force * dinv_ref[...] + correction) * (1.0 / size)
    base_ref[...] = base
    field_ref[...] = operator(base, scale_ref, mass_ref, first_ref, second_ref)
    table = scatter_points(field_ref, slot_ref, hot_ref)
    newsums_ref[...] = table
    rows = send_lists(table, split_ref, curve_ref, hot_ref)
    if last:
        for t in range(LISTS):
            refs[t][...] = rows[t]
        return
    pay_ref, rows_ref = refs
    for t in range(2, LISTS):
        rows_ref[t - 2 : t - 1, :] = rows[t]
    gather_points(table, slot_ref, hot_ref, field_ref)
    line = coarse_line(field_ref[...] * minv_ref[...], phi_ref, pick_ref)
    image = image_of(line, entry_ref[...], xhot_ref[...])
    owner = owner_mask()
    for t in range(LISTS):
        loads = jnp.sum(weight_ref[t] * rows[t], axis=1, keepdims=True)
        line = jnp.sum(jnp.where(owner, loads, 0.0), axis=0, keepdims=True) * nline_ref[t : t + 1, :]
        image = image + image_of(line, nentry_ref[t : t + 1, :], nhot_ref[:, t * ENTRIES : (t + 1) * ENTRIES])
    write_payload(pay_ref, image, rows)


def after_split(got_ref, rows_ref, pay_ref, shalo_ref):
    here, size = lax.axis_index("split"), got_ref.shape[0]
    for t, offset in enumerate((-1, 1)):
        there = here + offset
        row = got_ref[jnp.clip(there, 0, size - 1), 0:1, CHUNK:]
        shalo_ref[t : t + 1, :] = jnp.where(jnp.logical_and(there >= 0, there < size), row, jnp.zeros((1, LO), F32))
    chunk = got_ref[0, 0:1, :CHUNK]
    for g in range(1, size):
        chunk = chunk + got_ref[g, 0:1, :CHUNK]
    wide = jnp.concatenate([chunk, jnp.zeros((1, LO), F32)], axis=1)
    here, size = lax.axis_index("curve"), pay_ref.shape[0]
    for g in range(size):
        pay_ref[g] = wide
    for t, offset in enumerate((-2, -1, 1, 2)):
        there = here + offset

        @pl.when(jnp.logical_and(there >= 0, there < size))
        def _():
            pay_ref[jnp.clip(there, 0, size - 1), 0:1, CHUNK:] = rows_ref[t : t + 1, :]


def after_curve(got_ref, pay_ref, chalo_ref):
    here, size = lax.axis_index("curve"), got_ref.shape[0]
    for t, offset in enumerate((-2, -1, 1, 2)):
        there = here + offset
        row = got_ref[jnp.clip(there, 0, size - 1), 0:1, CHUNK:]
        chalo_ref[t : t + 1, :] = jnp.where(jnp.logical_and(there >= 0, there < size), row, jnp.zeros((1, LO), F32))
    sums = [got_ref[g, 0:1, :CHUNK] for g in range(4)]
    for g in range(4, size):
        sums[g % 4] = sums[g % 4] + got_ref[g, 0:1, :CHUNK]
    chunk = (sums[0] + sums[1]) + (sums[2] + sums[3])
    for g in range(pay_ref.shape[0]):
        pay_ref[g] = chunk


def gram(*refs):
    slot_ref, split_ref, curve_ref, hot_ref, sums_ref, minv_ref, right_ref = refs[:7]
    base_refs, force_refs, in_refs = refs[7:11], refs[11:14], refs[14:20]
    last_ref, pay_ref = refs[20:]
    rows = [ref[...] for ref in in_refs]
    gather_points(
        sums_ref[...] + incoming_table(split_ref, curve_ref, hot_ref, rows), slot_ref, hot_ref, last_ref
    )
    weighted = [ref[...] * minv_ref[...] for ref in base_refs]
    scalars = []
    for ref in (right_ref, *force_refs, last_ref):
        scalars += [total(ref[...] * base) for base in weighted]
    row = place(scalars)
    for g in range(pay_ref.shape[0]):
        pay_ref[g] = row


def finish(*refs):
    got_ref, norm_ref, right_ref = refs[:3]
    base_refs, force_refs = refs[3:7], refs[7:11]
    solution_ref, residual_ref = refs[11:]
    sums = [got_ref[g] for g in range(8)]
    for g in range(8, got_ref.shape[0]):
        sums[g % 8] = sums[g % 8] + got_ref[g]
    row = ((sums[0] + sums[1]) + (sums[2] + sums[3])) + ((sums[4] + sums[5]) + (sums[6] + sums[7]))
    table = [[row[:, 4 * i + j : 4 * i + j + 1] for j in range(4)] for i in range(5)]
    norms = [norm_ref[0:1, j : j + 1] for j in range(4)]

    def pair(left, right):
        acc = None
        for i, a in enumerate(left):
            inner = None
            for j, b in enumerate(right):
                if b is not None:
                    inner = b * table[i][j] if inner is None else inner + b * table[i][j]
            if a is not None and inner is not None:
                acc = a * inner if acc is None else acc + a * inner
        return acc

    def less(value, factor, other):
        if other is None:
            return value
        return -factor * other if value is None else value - factor * other

    residual = [jnp.ones((1, 1), F32)] + [None] * 4
    precond = [norms[0]] + [None] * 3
    direction = list(precond)
    solution = [None] * 4
    rz = pair(residual, precond)
    for k in range(ITERS):
        moved = [None] + direction
        alpha = rz / pair(moved, direction)
        solution = [less(value, -alpha, other) for value, other in zip(solution, direction)]
        residual = [less(value, alpha, other) for value, other in zip(residual, moved)]
        if k < ITERS - 1:
            shifted = [None] + [None if d is None else d * norms[j + 1] for j, d in enumerate(direction[:3])]
            precond = [less(value, alpha, other) for value, other in zip(precond, shifted)]
            rz_next = pair(residual, precond)
            beta = rz_next / rz
            direction = [less(value, -beta, other) for value, other in zip(precond, direction)]
            rz = rz_next
    result = solution[0] * base_refs[0][...]
    for j in range(1, 4):
        result = result + solution[j] * base_refs[j][...]
    solution_ref[...] = result
    result = right_ref[...]
    for j in range(4):
        result = result + residual[j + 1] * force_refs[j][...]
    residual_ref[...] = result


def run(body, name, args, outs, scratch=()):
    return pl.pallas_call(
        body,
        name=name,
        out_shape=[jax.ShapeDtypeStruct(shape, dtype) for shape, dtype in outs],
        in_specs=[pl.BlockSpec(memory_space=pltpu.VMEM) for _ in args],
        out_specs=[pl.BlockSpec(memory_space=pltpu.VMEM) for _ in outs],
        scratch_shapes=list(scratch),
        compiler_params=pltpu.CompilerParams(vmem_limit_bytes=VMEM_LIMIT),
    )(*args)


def shift(block, axis, offset):
    size = lax.axis_size(axis)
    route = [(i, i + offset) for i in range(size) if 0 <= i + offset < size]
    return lax.ppermute(block, axis, route)


WAYS = (("split", -1), ("split", 1), ("curve", -2), ("curve", -1), ("curve", 1), ("curve", 2))


def exchange(outgoing):
    arrived = [None] * LISTS
    for t, (axis, offset) in enumerate(WAYS):
        back = WAYS.index((axis, -offset))
        arrived[back] = shift(outgoing[t], axis, offset)
    return arrived


def reduce_image(pay, rows):
    splits, curves = lax.axis_size("split"), lax.axis_size("curve")
    got = lax.all_to_all(pay, "split", 0, 0)
    pay, shalo = run(
        after_split, "after_split", (got, rows), [((curves, 1, CHUNK + LO), F32), ((2, LO), F32)]
    )
    got = lax.all_to_all(pay, "curve", 0, 0)
    pay, chalo = run(after_curve, "after_curve", (got,), [((splits, 1, CHUNK), F32), ((4, LO), F32)])
    return lax.all_to_all(pay, "split", 0, 0), shalo, chalo


def local(rhs_load, stretch, helm_shift, local_slot, share_curve, share_split, coarse_slot, x_vals, x_cols, x_count):
    mass, first, second, diags, coarse = element_tables()
    mass = jnp.asarray(mass.reshape(1, -1), F32)
    diags = jnp.asarray(diags, F32)
    phi = jnp.asarray(coarse, F32)
    first = jnp.asarray(table_pieces(first))
    second = jnp.asarray(table_pieces(second))
    field = ((ELEMS, POINTS), F32)
    table = ((HI, LO), F32)
    line = ((1, LO), F32)
    payload = [((8, 1, CHUNK + LO), F32), ((4, LO), F32)]
    entry = jnp.int32

    hot, sums3, scale, _, entries, pick, xhot, *sent = run(
        setup_scatter,
        "setup_scatter",
        (rhs_load, local_slot, share_split, share_curve, stretch, helm_shift.reshape(1, -1), coarse_slot, x_vals,
         x_cols, x_count.reshape(1, -1), mass, diags, phi),
        [((LO, WIDE + LISTS * LO), BF16), ((3, HI, LO), F32), ((ELEMS, 8), F32), ((1, ENTRIES), F32),
         ((1, ENTRIES), entry), ((8, ELEMS, ENTRIES), F32), ((LO, ENTRIES), BF16)] + [((24, LO), F32)] * LISTS,
    )
    arrived = exchange(sent)
    shape = (local_slot, share_split, share_curve, hot)
    minv, dinv, right, nline, nentry, nhot, pay, rows = run(
        setup_gather,
        "setup_gather",
        (*shape, sums3, phi, pick, entries, xhot, *arrived),
        [field, field, field, ((LISTS, ENTRIES), F32), ((LISTS, ENTRIES), entry), ((LO, LISTS * ENTRIES), BF16)]
        + payload,
    )
    common = (*shape, scale, mass, first, second, phi, pick, entries, xhot, nline, nentry, nhot, minv, dinv)
    scratch = [pltpu.VMEM((ROWS, LO), F32), pltpu.VMEM((ELEMS, POINTS), F32)]
    norm = jnp.ones((1, LO), F32)
    bases, forces = [], []
    for index in range(ITERS):
        last = index == ITERS - 1
        gathered, shalo, chalo = reduce_image(pay, rows)
        own = (right, *arrived) if index == 0 else (weight, sums)
        outs = [field, line, table] + [((LISTS, ELEMS, LO), F32) if index == 0 else field]
        base, norm, sums, extra, *rest = run(
            functools.partial(krylov_step, index, last),
            f"krylov_step{index}",
            (*common, norm, gathered, shalo, chalo, *own),
            outs + ([line] * LISTS if last else payload),
            scratch,
        )
        bases.append(base)
        if index == 0:
            weight = extra
        else:
            forces.append(extra)
        if not last:
            pay, rows = rest
    devices = lax.axis_size("curve") * lax.axis_size("split")
    force, pay = run(
        gram,
        "gram",
        (*shape, sums, minv, right, *bases, *forces, *exchange(rest)),
        [field, ((devices, 1, LO), F32)],
    )
    got = lax.all_to_all(pay, ("curve", "split"), 0, 0)
    solution, residual = run(
        finish, "finish", (got, norm, right, *bases, *forces, force), [field, field]
    )
    return solution, residual


def solution(mesh):
    in_specs = (
        P(("curve", "split"), None),
        P(None, ("curve", "split")),
        P(("curve", "split")),
        P(("curve", "split"), None),
        P("curve", "split", None, None),
        P("curve", "split", None, None),
        P(None, ("curve", "split")),
        P(None, ("curve", "split")),
        P(None, ("curve", "split")),
        P(("curve", "split")),
    )
    out_specs = (P(("curve", "split"), None), P(("curve", "split"), None))
    return jax.shard_map(local, mesh=mesh, in_specs=in_specs, out_specs=out_specs, check_vma=False)
```

```python
import functools

import jax
import jax.numpy as jnp
import ml_dtypes
import numpy as np
from jax import lax
from jax.experimental import pallas as pl
from jax.experimental.pallas import tpu as pltpu
from jax.sharding import PartitionSpec as P

ITERS = 4
HI = 48
LO = 128
ELEMS = 16
POINTS = 512
LISTS = 6
WIDE = ELEMS * POINTS
ENTRIES = 256
ROWS = 64
CHUNK = 1024
PIECES = 2
F32 = jnp.float32
BF16 = jnp.bfloat16
VMEM_LIMIT = 16 << 20


def element_tables():
    poly_order = 7
    node_count = poly_order + 1
    nodes = -np.cos(np.pi * np.arange(node_count) / poly_order)
    legendre = np.zeros((node_count, node_count))

    def fill():
        legendre[:, 0] = 1.0
        legendre[:, 1] = nodes
        for degree in range(2, node_count):
            legendre[:, degree] = (
                (2 * degree - 1) * nodes * legendre[:, degree - 1] - (degree - 1) * legendre[:, degree - 2]
            ) / degree

    for _ in range(60):
        fill()
        nodes = nodes - (nodes * legendre[:, poly_order] - legendre[:, poly_order - 1]) / (
            node_count * legendre[:, poly_order]
        )
    fill()
    top = legendre[:, poly_order]
    weights = 2.0 / (poly_order * node_count * top * top)
    deriv = np.zeros((node_count, node_count))
    for i in range(node_count):
        for j in range(node_count):
            if i != j:
                deriv[i, j] = top[i] / (top[j] * (nodes[i] - nodes[j]))
    deriv[0, 0] = -poly_order * node_count / 4.0
    deriv[poly_order, poly_order] = poly_order * node_count / 4.0
    mass = (weights[:, None, None] * weights[None, :, None] * weights[None, None, :]).reshape(-1)
    line = deriv.T @ (weights[:, None] * deriv)
    scaled = line / weights[None, :]
    eye = np.eye(node_count)
    first = np.kron(scaled, np.eye(64))
    second = np.kron(np.eye(4), np.kron(scaled, eye))
    third = np.kron(np.eye(4), np.kron(eye, scaled))
    diag = np.diag(scaled)
    ones = np.ones(node_count)
    diags = np.stack(
        [
            mass * np.kron(diag, np.kron(ones, ones)),
            mass * np.kron(ones, np.kron(diag, ones)),
            mass * np.kron(ones, np.kron(ones, diag)),
        ]
    )
    hats = np.stack([(1.0 - nodes) / 2.0, (1.0 + nodes) / 2.0])
    coarse = (
        hats[:, None, None, :, None, None]
        * hats[None, :, None, None, :, None]
        * hats[None, None, :, None, None, :]
    ).reshape(8, -1)
    return mass, first, np.concatenate([second, third], axis=1), diags, coarse


def table_pieces(table):
    rest = np.asarray(table, np.float32)
    pieces = []
    for _ in range(PIECES):
        piece = rest.astype(ml_dtypes.bfloat16)
        pieces.append(piece)
        rest = rest - piece.astype(np.float32)
    return np.stack(pieces)


def pieces(value):
    found = []
    for left in reversed(range(PIECES)):
        found.append(value.astype(BF16))
        if left:
            value = value - found[-1].astype(F32)
    return found


def row_mask(slots, height):
    high = lax.shift_right_logical(slots, 7)
    width = slots.shape[1]
    return jnp.broadcast_to(high, (height, width)) == lax.broadcasted_iota(jnp.int32, (height, width), 0)


def lane_hot(slots):
    low = lax.bitwise_and(slots, LO - 1)
    width = slots.shape[1]
    hot = jnp.broadcast_to(low, (LO, width)) == lax.broadcasted_iota(jnp.int32, (LO, width), 0)
    return jnp.where(hot, 1.0, 0.0).astype(BF16)


def spread(values, mask):
    wide = [jnp.where(mask, jnp.broadcast_to(value, mask.shape), 0.0) for value in values]
    return jnp.concatenate([piece for value in wide for piece in pieces(value)], axis=0)


def put(left, hot):
    return lax.dot_general(left, hot, (((1,), (1,)), ((), ())), preferred_element_type=F32)


def table_parts(table):
    return jnp.concatenate(pieces(table), axis=1)


def take(parts, hot, mask):
    found = jnp.dot(parts, jnp.concatenate([hot] * PIECES, axis=0), preferred_element_type=F32)
    return jnp.sum(jnp.where(mask, found, 0.0), axis=0, keepdims=True)


def fold(stacked, height):
    result = stacked[:height]
    for piece in range(1, PIECES):
        result = result + stacked[piece * height : (piece + 1) * height]
    return result


def total(value):
    return jnp.sum(jnp.sum(value, axis=1, keepdims=True), axis=0, keepdims=True)


def place(scalars):
    lane = lax.broadcasted_iota(jnp.int32, (1, LO), 1)
    row = jnp.zeros((1, LO), F32)
    for index, scalar in enumerate(scalars):
        row = jnp.where(lane == index, scalar, row)
    return row


def column(row):
    size = row.shape[1]
    square = lax.broadcasted_iota(jnp.int32, (size, size), 0) == lax.broadcasted_iota(jnp.int32, (size, size), 1)
    return jnp.sum(jnp.where(square, jnp.broadcast_to(row, (size, size)), 0.0), axis=1, keepdims=True)


def flatten(square):
    lane = lax.broadcasted_iota(jnp.int32, (16, ENTRIES), 1)
    sub = lax.broadcasted_iota(jnp.int32, (16, ENTRIES), 0)
    spreader = jnp.where(lax.bitwise_and(lane, 15) == sub, 1.0, 0.0)
    wide = jnp.dot(square, spreader, precision=lax.Precision.HIGHEST, preferred_element_type=F32)
    return jnp.sum(jnp.where(lax.shift_right_logical(lane, 4) == sub, wide, 0.0), axis=0, keepdims=True)


def list_row(split_ref, curve_ref, t):
    return split_ref[0, 0, t : t + 1, :] if t < 2 else curve_ref[0, 0, t - 2 : t - 1, :]


def list_hot(hot_ref, t):
    return hot_ref[:, WIDE + t * LO : WIDE + (t + 1) * LO]


def point_hot(hot_ref, e):
    return hot_ref[:, e * POINTS : (e + 1) * POINTS]


def owner_mask():
    lane = lax.broadcasted_iota(jnp.int32, (ELEMS, ENTRIES), 1)
    return lax.bitwise_and(lane, 15) == lax.broadcasted_iota(jnp.int32, (ELEMS, ENTRIES), 0)


def coarse_line(scaled, phi_ref, pick_ref):
    acc = jnp.zeros((ELEMS, ENTRIES), F32)
    for v in range(8):
        restricted = jnp.sum(scaled * phi_ref[v : v + 1, :], axis=1, keepdims=True)
        acc = acc + restricted * pick_ref[v]
    return jnp.sum(acc, axis=0, keepdims=True)


def coarse_correction(image, phi_ref, pick_ref, xcols, xhot):
    line = take(table_parts(image), xhot, row_mask(xcols, ROWS))
    result = jnp.zeros((ELEMS, POINTS), F32)
    for v in range(8):
        vertex = jnp.sum(pick_ref[v] * line, axis=1, keepdims=True)
        result = result + vertex * phi_ref[v : v + 1, :]
    return result


def image_of(line, cols, hot):
    return fold(put(spread([line], row_mask(cols, ROWS)), hot), ROWS)


def write_payload(pay_ref, image, rows):
    here = lax.axis_index("split")
    for g in range(8):
        for r in range(8):
            pay_ref[g, 0:1, r * LO : (r + 1) * LO] = image[8 * g + r : 8 * g + r + 1, :]
        row = jnp.where(here == g + 1, rows[0], jnp.where(here == g - 1, rows[1], jnp.zeros((1, LO), F32)))
        pay_ref[g, 0:1, CHUNK:] = row


def setup_scatter(*refs):
    sources, refs = refs[:15], refs[15:]
    slot_ref, split_ref, curve_ref, mass_ref, phi_ref, first_ref, second_ref = refs[:7]
    hot_ref, sums_ref, scale_ref, entry_ref, pick_ref, xhot_ref = refs[7:13]
    out_refs = refs[13:19]
    rhs_ref, stretch_ref, helm_ref, corner_ref, xvals_ref, xcols_ref, xcount_ref, diag_ref, sems = refs[19:]
    targets = (rhs_ref, stretch_ref, helm_ref, corner_ref, xvals_ref, xcols_ref, xcount_ref, diag_ref) + refs[:7]
    copies = [pltpu.make_async_copy(a, b, sems.at[i]) for i, (a, b) in enumerate(zip(sources, targets))]
    for copy in copies:
        copy.start()
    for copy in copies:
        copy.wait()
    columns = [column(stretch_ref[d : d + 1, :]) for d in range(3)] + [column(helm_ref[...])]
    scale_ref[...] = jnp.concatenate(columns + columns, axis=1)
    diag = columns[3] * mass_ref[...]
    for d in range(3):
        diag = diag + columns[d] * diag_ref[d : d + 1, :]
    live = lax.broadcasted_iota(jnp.int32, (16, 16), 0) < jnp.broadcast_to(xcount_ref[...], (16, 16))
    factor = flatten(jnp.where(live, xvals_ref[...], 0.0))
    cols = flatten(xcols_ref[...].astype(F32))
    entries = (cols + 0.5).astype(jnp.int32)
    entry_ref[...] = entries
    xhot_ref[...] = lane_hot(entries)
    owner = lax.bitwise_and(lax.broadcasted_iota(jnp.int32, (ELEMS, ENTRIES), 1), 15)
    corners = [column(corner_ref[v : v + 1, :].astype(F32)) for v in range(8)]
    for v in range(8):
        pick_ref[v] = jnp.where((corners[v] + 0.5).astype(jnp.int32) == owner, factor, 0.0)
    corner = jnp.concatenate(corners, axis=1)
    lists = jnp.concatenate(
        [column(list_row(split_ref, curve_ref, t).astype(F32)) for t in range(LISTS)], axis=0
    )
    lists = (lists + 0.5).astype(jnp.int32)
    acc = jnp.zeros(((1 + 2 * PIECES) * HI, LO), F32)
    weights = jnp.zeros((PIECES * ELEMS, LISTS * LO), F32)
    for e in range(ELEMS):
        slots = slot_ref[e : e + 1, :]
        hot = lane_hot(slots)
        hot_ref[:, e * POINTS : (e + 1) * POINTS] = hot
        mask = row_mask(slots, HI)
        left = spread([diag[e : e + 1, :], rhs_ref[e : e + 1, :]], mask)
        left = jnp.concatenate([jnp.where(mask, 1.0, 0.0).astype(BF16), left], axis=0)
        acc = acc + put(left, hot)
        unknown = lax.broadcasted_iota(jnp.int32, (ELEMS, 8), 0).astype(F32)
        vertex = jnp.where(jnp.abs(corner[e : e + 1, :] - unknown) < 0.5, 1.0, 0.0)
        basis = jnp.dot(vertex, phi_ref[...], precision=lax.Precision.HIGHEST, preferred_element_type=F32)
        shape = (LISTS * LO, POINTS)
        same = jnp.where(jnp.broadcast_to(slots, shape) == jnp.broadcast_to(lists, shape), 1.0, 0.0)
        weights = weights + put(jnp.concatenate(pieces(basis), axis=0), same.astype(BF16))
    weights = fold(weights, ELEMS)
    tables = []
    for field in range(3):
        first = HI + PIECES * HI * (field - 1)
        table = fold(acc[first : first + PIECES * HI], HI) if field else acc[:HI]
        sums_ref[field] = table
        tables.append(table_parts(table))
    for t in range(LISTS):
        slots = list_row(split_ref, curve_ref, t)
        hot = lane_hot(slots)
        hot_ref[:, WIDE + t * LO : WIDE + (t + 1) * LO] = hot
        mask = row_mask(slots, HI)
        rows = [take(tables[field], hot, mask) for field in range(3)]
        rows += [cols[:, :LO], cols[:, LO:], factor[:, :LO], factor[:, LO:], jnp.zeros((1, LO), F32)]
        for r in range(8):
            out_refs[t][r : r + 1, :] = rows[r]
        out_refs[t][8:24, :] = weights[:, t * LO : (t + 1) * LO]


def incoming_table(split_ref, curve_ref, hot_ref, rows):
    acc = jnp.zeros((PIECES * HI, LO), F32)
    for t in range(LISTS):
        mask = row_mask(list_row(split_ref, curve_ref, t), HI)
        acc = acc + put(spread([rows[t]], mask), list_hot(hot_ref, t))
    return fold(acc, HI)


def setup_gather(slot_ref, split_ref, curve_ref, hot_ref, sums_ref, phi_ref, pick_ref, entry_ref, xhot_ref, *refs):
    in_refs = refs[:LISTS]
    minv_ref, dinv_ref, right_ref, nline_ref, nentry_ref, nhot_ref, pay_ref, rows_ref = refs[LISTS:]
    tables = [
        table_parts(
            sums_ref[field] + incoming_table(split_ref, curve_ref, hot_ref, [ref[field : field + 1, :] for ref in in_refs])
        )
        for field in range(3)
    ]
    for e in range(ELEMS):
        mask = row_mask(slot_ref[e : e + 1, :], HI)
        hot = point_hot(hot_ref, e)
        minv_ref[e : e + 1, :] = 1.0 / take(tables[0], hot, mask)
        dinv_ref[e : e + 1, :] = 1.0 / take(tables[1], hot, mask)
        right_ref[e : e + 1, :] = take(tables[2], hot, mask)
    rows = []
    for t in range(LISTS):
        mult = take(tables[0], list_hot(hot_ref, t), row_mask(list_row(split_ref, curve_ref, t), HI))
        rows.append(jnp.where(mult > 0.5, 1.0 / jnp.where(mult > 0.5, mult, 1.0), 0.0))
        there = jnp.concatenate([in_refs[t][3:4, :], in_refs[t][4:5, :]], axis=1)
        entries = (there + 0.5).astype(jnp.int32)
        nentry_ref[t : t + 1, :] = entries
        nhot_ref[:, t * ENTRIES : (t + 1) * ENTRIES] = lane_hot(entries)
        nline_ref[t : t + 1, :] = jnp.concatenate([in_refs[t][5:6, :], in_refs[t][6:7, :]], axis=1)
    for t in range(2, LISTS):
        rows_ref[t - 2 : t - 1, :] = rows[t]
    line = coarse_line(right_ref[...] * minv_ref[...], phi_ref, pick_ref)
    write_payload(pay_ref, image_of(line, entry_ref[...], xhot_ref[...]), rows)


def operator(u, scale_ref, mass_ref, first_ref, second_ref):
    def product(parts, ref):
        rows = parts[0].shape[0]
        one = jnp.dot(jnp.concatenate(parts, axis=0), ref[0], preferred_element_type=F32)
        return one[:rows] + (one[rows:] + jnp.dot(parts[0], ref[1], preferred_element_type=F32))

    half = POINTS // 2
    parts = pieces(u)
    along = product(parts, first_ref)
    inside = product([jnp.concatenate([p[:, :half], p[:, half:]], axis=0) for p in parts], second_ref)
    second = jnp.concatenate([inside[:ELEMS, :half], inside[ELEMS:, :half]], axis=1)
    third = jnp.concatenate([inside[:ELEMS, half:], inside[ELEMS:, half:]], axis=1)
    result = scale_ref[:, 0:1] * along + scale_ref[:, 1:2] * second + scale_ref[:, 2:3] * third
    return mass_ref[...] * (result + scale_ref[:, 3:4] * u)


def scatter_points(field_ref, slot_ref, hot_ref):
    acc = jnp.zeros((PIECES * HI, LO), F32)
    for e in range(ELEMS):
        left = spread([field_ref[e : e + 1, :]], row_mask(slot_ref[e : e + 1, :], HI))
        acc = acc + put(left, point_hot(hot_ref, e))
    return fold(acc, HI)


def gather_points(table, slot_ref, hot_ref, out_ref):
    parts = table_parts(table)
    for e in range(ELEMS):
        out_ref[e : e + 1, :] = take(parts, point_hot(hot_ref, e), row_mask(slot_ref[e : e + 1, :], HI))


def send_lists(table, split_ref, curve_ref, hot_ref):
    parts = table_parts(table)
    return [
        take(parts, list_hot(hot_ref, t), row_mask(list_row(split_ref, curve_ref, t), HI)) for t in range(LISTS)
    ]


def halo_rows(shalo_ref, chalo_ref):
    return [shalo_ref[t : t + 1, :] for t in range(2)] + [chalo_ref[t : t + 1, :] for t in range(4)]


def coarse_shift(image, earlier):
    factors = []
    for other in earlier:
        size = total(other * other)
        fits = size > 1e-30
        factors.append(jnp.where(fits, total(image * other) / jnp.where(fits, size, 1.0), 0.0))
    for factor, other in zip(factors, earlier):
        image = image - factor * other
    return factors, image


def krylov_step(index, last, *refs):
    (slot_ref, split_ref, curve_ref, hot_ref, scale_ref, mass_ref, first_ref, second_ref, phi_ref, pick_ref,
     entry_ref, xhot_ref, nline_ref, nentry_ref, nhot_ref, minv_ref, dinv_ref, norm_ref, gathered_ref,
     shalo_ref, chalo_ref) = refs[:21]
    refs = refs[21:]
    image_ref, field_ref = refs[-2:]
    refs = refs[:-2]
    rows = halo_rows(shalo_ref, chalo_ref)
    if index == 0:
        right_ref, *sent_refs = refs[:7]
        refs = refs[7:]
        force = right_ref[...]
    else:
        weight_ref, sums_ref = refs[:2]
        refs = refs[2:]
        olds, refs = refs[: 2 * index], refs[2 * index :]
        base_refs, coarse_refs = olds[:index], olds[index:]
    base_ref, newnorm_ref, newsums_ref = refs[:3]
    refs = refs[3:]
    if index == 0:
        newweight_ref = refs[0]
        refs = refs[1:]
        for t in range(LISTS):
            newweight_ref[t] = sent_refs[t][8:24, :] * rows[t]
        weight_ref = newweight_ref
    else:
        force_ref = refs[0]
        refs = refs[1:]
        gather_points(
            sums_ref[...] + incoming_table(split_ref, curve_ref, hot_ref, rows), slot_ref, hot_ref, force_ref
        )
        force = force_ref[...]
    for g in range(8):
        for r in range(8):
            image_ref[8 * g + r : 8 * g + r + 1, :] = gathered_ref[g, 0:1, r * LO : (r + 1) * LO]
    image = image_ref[...]
    correction = coarse_correction(image, phi_ref, pick_ref, entry_ref[...], xhot_ref[...])
    base = force * dinv_ref[...] + correction
    if index:
        factors, image = coarse_shift(image, [ref[...] for ref in coarse_refs])
        for factor, ref in zip(factors, base_refs):
            base = base - factor * ref[...]
    else:
        factors = []
    size = 1.0 + jnp.sqrt(total(image * image))
    base = base * (1.0 / size)
    base_ref[...] = base
    if not last:
        coarse_ref, *refs = refs
        coarse_ref[...] = image * (1.0 / size)
    newnorm_ref[...] = norm_ref[...]
    newnorm_ref[index : index + 1, :] = place(factors + [size])
    field_ref[...] = operator(base, scale_ref, mass_ref, first_ref, second_ref)
    table = scatter_points(field_ref, slot_ref, hot_ref)
    newsums_ref[...] = table
    rows = send_lists(table, split_ref, curve_ref, hot_ref)
    if last:
        for t in range(LISTS):
            refs[t][...] = rows[t]
        return
    pay_ref, rows_ref = refs
    for t in range(2, LISTS):
        rows_ref[t - 2 : t - 1, :] = rows[t]
    gather_points(table, slot_ref, hot_ref, field_ref)
    line = coarse_line(field_ref[...] * minv_ref[...], phi_ref, pick_ref)
    image = image_of(line, entry_ref[...], xhot_ref[...])
    owner = owner_mask()
    for t in range(LISTS):
        loads = jnp.sum(weight_ref[t] * rows[t], axis=1, keepdims=True)
        line = jnp.sum(jnp.where(owner, loads, 0.0), axis=0, keepdims=True) * nline_ref[t : t + 1, :]
        image = image + image_of(line, nentry_ref[t : t + 1, :], nhot_ref[:, t * ENTRIES : (t + 1) * ENTRIES])
    write_payload(pay_ref, image, rows)


def after_split(got_ref, rows_ref, pay_ref, shalo_ref):
    here, size = lax.axis_index("split"), got_ref.shape[0]
    for t, offset in enumerate((-1, 1)):
        there = here + offset
        row = got_ref[jnp.clip(there, 0, size - 1), 0:1, CHUNK:]
        shalo_ref[t : t + 1, :] = jnp.where(jnp.logical_and(there >= 0, there < size), row, jnp.zeros((1, LO), F32))
    chunk = got_ref[0, 0:1, :CHUNK]
    for g in range(1, size):
        chunk = chunk + got_ref[g, 0:1, :CHUNK]
    wide = jnp.concatenate([chunk, jnp.zeros((1, LO), F32)], axis=1)
    here, size = lax.axis_index("curve"), pay_ref.shape[0]
    for g in range(size):
        pay_ref[g] = wide
    for t, offset in enumerate((-2, -1, 1, 2)):
        there = here + offset

        @pl.when(jnp.logical_and(there >= 0, there < size))
        def _():
            pay_ref[jnp.clip(there, 0, size - 1), 0:1, CHUNK:] = rows_ref[t : t + 1, :]


def after_curve(got_ref, pay_ref, chalo_ref):
    here, size = lax.axis_index("curve"), got_ref.shape[0]
    for t, offset in enumerate((-2, -1, 1, 2)):
        there = here + offset
        row = got_ref[jnp.clip(there, 0, size - 1), 0:1, CHUNK:]
        chalo_ref[t : t + 1, :] = jnp.where(jnp.logical_and(there >= 0, there < size), row, jnp.zeros((1, LO), F32))
    sums = [got_ref[g, 0:1, :CHUNK] for g in range(4)]
    for g in range(4, size):
        sums[g % 4] = sums[g % 4] + got_ref[g, 0:1, :CHUNK]
    chunk = (sums[0] + sums[1]) + (sums[2] + sums[3])
    for g in range(pay_ref.shape[0]):
        pay_ref[g] = chunk


def gram(*refs):
    slot_ref, split_ref, curve_ref, hot_ref, sums_ref, minv_ref, right_ref = refs[:7]
    base_refs, force_refs, in_refs = refs[7:11], refs[11:14], refs[14:20]
    last_ref, pay_ref = refs[20:]
    rows = [ref[...] for ref in in_refs]
    gather_points(
        sums_ref[...] + incoming_table(split_ref, curve_ref, hot_ref, rows), slot_ref, hot_ref, last_ref
    )
    weighted = [ref[...] * minv_ref[...] for ref in base_refs]
    scalars = []
    for ref in (right_ref, *force_refs, last_ref):
        scalars += [total(ref[...] * base) for base in weighted]
    row = place(scalars)
    for g in range(pay_ref.shape[0]):
        pay_ref[g] = row


def finish(*refs):
    got_ref, norm_ref, right_ref = refs[:3]
    base_refs, force_refs = refs[3:7], refs[7:11]
    solution_ref, residual_ref = refs[11:]
    sums = [got_ref[g] for g in range(8)]
    for g in range(8, got_ref.shape[0]):
        sums[g % 8] = sums[g % 8] + got_ref[g]
    row = ((sums[0] + sums[1]) + (sums[2] + sums[3])) + ((sums[4] + sums[5]) + (sums[6] + sums[7]))
    table = [[row[:, 4 * i + j : 4 * i + j + 1] for j in range(4)] for i in range(5)]
    relation = [[norm_ref[i : i + 1, j : j + 1] for j in range(i + 1)] for i in range(4)]

    def pair(left, right):
        acc = None
        for i, a in enumerate(left):
            inner = None
            for j, b in enumerate(right):
                if b is not None:
                    inner = b * table[i][j] if inner is None else inner + b * table[i][j]
            if a is not None and inner is not None:
                acc = a * inner if acc is None else acc + a * inner
        return acc

    def less(value, factor, other):
        if other is None:
            return value
        return -factor * other if value is None else value - factor * other

    residual = [jnp.ones((1, 1), F32)] + [None] * 4
    precond = [relation[0][0]] + [None] * 3
    direction = list(precond)
    solution = [None] * 4
    rz = pair(residual, precond)
    for k in range(ITERS):
        moved = [None] + direction
        alpha = rz / pair(moved, direction)
        solution = [less(value, -alpha, other) for value, other in zip(solution, direction)]
        residual = [less(value, alpha, other) for value, other in zip(residual, moved)]
        if k < ITERS - 1:
            shifted = [None] * 4
            for j, d in enumerate(direction[:3]):
                if d is not None:
                    for i, factor in enumerate(relation[j + 1]):
                        shifted[i] = less(shifted[i], -d, factor)
            precond = [less(value, alpha, other) for value, other in zip(precond, shifted)]
            rz_next = pair(residual, precond)
            beta = rz_next / rz
            direction = [less(value, -beta, other) for value, other in zip(precond, direction)]
            rz = rz_next
    result = solution[0] * base_refs[0][...]
    for j in range(1, 4):
        result = result + solution[j] * base_refs[j][...]
    solution_ref[...] = result
    result = right_ref[...]
    for j in range(4):
        result = result + residual[j + 1] * force_refs[j][...]
    residual_ref[...] = result


def run(body, name, args, outs, scratch=(), where=pltpu.VMEM):
    return pl.pallas_call(
        body,
        name=name,
        out_shape=[jax.ShapeDtypeStruct(shape, dtype) for shape, dtype in outs],
        in_specs=[pl.BlockSpec(memory_space=where) for _ in args],
        out_specs=[pl.BlockSpec(memory_space=pltpu.VMEM) for _ in outs],
        scratch_shapes=list(scratch),
        compiler_params=pltpu.CompilerParams(vmem_limit_bytes=VMEM_LIMIT),
    )(*args)


def shift(block, axis, offset):
    size = lax.axis_size(axis)
    route = [(i, i + offset) for i in range(size) if 0 <= i + offset < size]
    return lax.ppermute(block, axis, route)


WAYS = (("split", -1), ("split", 1), ("curve", -2), ("curve", -1), ("curve", 1), ("curve", 2))


def exchange(outgoing):
    arrived = [None] * LISTS
    for t, (axis, offset) in enumerate(WAYS):
        back = WAYS.index((axis, -offset))
        arrived[back] = shift(outgoing[t], axis, offset)
    return arrived


def reduce_image(pay, rows):
    splits, curves = lax.axis_size("split"), lax.axis_size("curve")
    got = lax.all_to_all(pay, "split", 0, 0)
    pay, shalo = run(
        after_split, "after_split", (got, rows), [((curves, 1, CHUNK + LO), F32), ((2, LO), F32)]
    )
    got = lax.all_to_all(pay, "curve", 0, 0)
    pay, chalo = run(after_curve, "after_curve", (got,), [((splits, 1, CHUNK), F32), ((4, LO), F32)])
    return lax.all_to_all(pay, "split", 0, 0), shalo, chalo


def local(rhs_load, stretch, helm_shift, local_slot, share_curve, share_split, coarse_slot, x_vals, x_cols, x_count):
    mass, first, second, diags, coarse = element_tables()
    mass = jnp.asarray(mass.reshape(1, -1), F32)
    diags = jnp.asarray(diags, F32)
    phi = jnp.asarray(coarse, F32)
    first = jnp.asarray(table_pieces(first))
    second = jnp.asarray(table_pieces(second))
    field = ((ELEMS, POINTS), F32)
    table = ((HI, LO), F32)
    line = ((1, LO), F32)
    payload = [((8, 1, CHUNK + LO), F32), ((4, LO), F32)]
    entry = jnp.int32

    sources = (rhs_load, stretch, helm_shift.reshape(1, -1), coarse_slot, x_vals, x_cols, x_count.reshape(1, -1), diags,
               local_slot, share_split, share_curve, mass, phi, first, second)
    kept = [(array.shape, array.dtype) for array in sources[8:]]
    outs = kept + [
        ((LO, WIDE + LISTS * LO), BF16), ((3, HI, LO), F32), ((ELEMS, 8), F32), ((1, ENTRIES), entry),
        ((8, ELEMS, ENTRIES), F32), ((LO, ENTRIES), BF16),
    ] + [((24, LO), F32)] * LISTS
    scratch = [pltpu.VMEM(array.shape, array.dtype) for array in sources[:8]]
    scratch.append(pltpu.SemaphoreType.DMA((len(sources),)))
    (local_slot, share_split, share_curve, mass, phi, first, second, hot, sums3, scale, entries, pick, xhot,
     *sent) = run(setup_scatter, "setup_scatter", tuple(pltpu.with_memory_space_constraint(a, pltpu.HBM) for a in sources), outs, scratch, pltpu.HBM)
    arrived = exchange(sent)
    shape = (local_slot, share_split, share_curve, hot)
    minv, dinv, right, nline, nentry, nhot, pay, rows = run(
        setup_gather,
        "setup_gather",
        (*shape, sums3, phi, pick, entries, xhot, *arrived),
        [field, field, field, ((LISTS, ENTRIES), F32), ((LISTS, ENTRIES), entry), ((LO, LISTS * ENTRIES), BF16)]
        + payload,
    )
    common = (*shape, scale, mass, first, second, phi, pick, entries, xhot, nline, nentry, nhot, minv, dinv)
    scratch = [pltpu.VMEM((ROWS, LO), F32), pltpu.VMEM((ELEMS, POINTS), F32)]
    norm = jnp.ones((8, LO), F32)
    bases, forces, coarses = [], [], []
    for index in range(ITERS):
        last = index == ITERS - 1
        gathered, shalo, chalo = reduce_image(pay, rows)
        own = (right, *arrived) if index == 0 else (weight, sums, *bases, *coarses)
        outs = [field, ((8, LO), F32), table] + [((LISTS, ELEMS, LO), F32) if index == 0 else field]
        outs += [] if last else [((ROWS, LO), F32)]
        base, norm, sums, extra, *rest = run(
            functools.partial(krylov_step, index, last),
            f"krylov_step{index}",
            (*common, norm, gathered, shalo, chalo, *own),
            outs + ([line] * LISTS if last else payload),
            scratch,
        )
        bases.append(base)
        if index == 0:
            weight = extra
        else:
            forces.append(extra)
        if not last:
            coarse, pay, rows = rest
            coarses.append(coarse)
    devices = lax.axis_size("curve") * lax.axis_size("split")
    force, pay = run(
        gram,
        "gram",
        (*shape, sums, minv, right, *bases, *forces, *exchange(rest)),
        [field, ((devices, 1, LO), F32)],
    )
    got = lax.all_to_all(pay, ("curve", "split"), 0, 0)
    solution, residual = run(
        finish, "finish", (got, norm, right, *bases, *forces, force), [field, field]
    )
    return solution, residual


def solution(mesh):
    in_specs = (
        P(("curve", "split"), None),
        P(None, ("curve", "split")),
        P(("curve", "split")),
        P(("curve", "split"), None),
        P("curve", "split", None, None),
        P("curve", "split", None, None),
        P(None, ("curve", "split")),
        P(None, ("curve", "split")),
        P(None, ("curve", "split")),
        P(("curve", "split")),
    )
    out_specs = (P(("curve", "split"), None), P(("curve", "split"), None))
    return jax.shard_map(local, mesh=mesh, in_specs=in_specs, out_specs=out_specs, check_vma=False)
```

```python
import functools

import jax
import jax.numpy as jnp
import ml_dtypes
import numpy as np
from jax import lax
from jax.experimental import pallas as pl
from jax.experimental.pallas import tpu as pltpu
from jax.sharding import PartitionSpec as P

ITERS = 4
HI = 48
LO = 128
ELEMS = 16
POINTS = 512
LISTS = 6
WIDE = ELEMS * POINTS
ENTRIES = 256
ROWS = 64
GROUP = 8
CHUNK = ROWS * LO // GROUP
PIECES = 2
F32 = jnp.float32
BF16 = jnp.bfloat16
VMEM_LIMIT = 16 << 20


def element_tables():
    poly_order = 7
    node_count = poly_order + 1
    nodes = -np.cos(np.pi * np.arange(node_count) / poly_order)
    legendre = np.zeros((node_count, node_count))

    def fill():
        legendre[:, 0] = 1.0
        legendre[:, 1] = nodes
        for degree in range(2, node_count):
            legendre[:, degree] = (
                (2 * degree - 1) * nodes * legendre[:, degree - 1] - (degree - 1) * legendre[:, degree - 2]
            ) / degree

    for _ in range(60):
        fill()
        nodes = nodes - (nodes * legendre[:, poly_order] - legendre[:, poly_order - 1]) / (
            node_count * legendre[:, poly_order]
        )
    fill()
    top = legendre[:, poly_order]
    weights = 2.0 / (poly_order * node_count * top * top)
    deriv = np.zeros((node_count, node_count))
    for i in range(node_count):
        for j in range(node_count):
            if i != j:
                deriv[i, j] = top[i] / (top[j] * (nodes[i] - nodes[j]))
    deriv[0, 0] = -poly_order * node_count / 4.0
    deriv[poly_order, poly_order] = poly_order * node_count / 4.0
    mass = (weights[:, None, None] * weights[None, :, None] * weights[None, None, :]).reshape(-1)
    line = deriv.T @ (weights[:, None] * deriv)
    scaled = line / weights[None, :]
    eye = np.eye(node_count)
    first = np.kron(scaled, np.eye(64))
    second = np.kron(np.eye(4), np.kron(scaled, eye))
    third = np.kron(np.eye(4), np.kron(eye, scaled))
    diag = np.diag(scaled)
    ones = np.ones(node_count)
    diags = np.stack(
        [
            mass * np.kron(diag, np.kron(ones, ones)),
            mass * np.kron(ones, np.kron(diag, ones)),
            mass * np.kron(ones, np.kron(ones, diag)),
        ]
    )
    hats = np.stack([(1.0 - nodes) / 2.0, (1.0 + nodes) / 2.0])
    coarse = (
        hats[:, None, None, :, None, None]
        * hats[None, :, None, None, :, None]
        * hats[None, None, :, None, None, :]
    ).reshape(8, -1)
    return mass, first, np.concatenate([second, third], axis=1), diags, coarse


def table_pieces(table):
    rest = np.asarray(table, np.float32)
    pieces = []
    for _ in range(PIECES):
        piece = rest.astype(ml_dtypes.bfloat16)
        pieces.append(piece)
        rest = rest - piece.astype(np.float32)
    return np.stack(pieces)


def pieces(value):
    found = []
    for left in reversed(range(PIECES)):
        found.append(value.astype(BF16))
        if left:
            value = value - found[-1].astype(F32)
    return found


def row_mask(slots, height):
    high = lax.shift_right_logical(slots, 7)
    width = slots.shape[1]
    return jnp.broadcast_to(high, (height, width)) == lax.broadcasted_iota(jnp.int32, (height, width), 0)


def lane_hot(slots):
    low = lax.bitwise_and(slots, LO - 1)
    width = slots.shape[1]
    hot = jnp.broadcast_to(low, (LO, width)) == lax.broadcasted_iota(jnp.int32, (LO, width), 0)
    return jnp.where(hot, 1.0, 0.0).astype(BF16)


def spread(values, mask):
    wide = [jnp.where(mask, jnp.broadcast_to(value, mask.shape), 0.0) for value in values]
    return jnp.concatenate([piece for value in wide for piece in pieces(value)], axis=0)


def put(left, hot):
    return lax.dot_general(left, hot, (((1,), (1,)), ((), ())), preferred_element_type=F32)


def table_parts(table):
    return jnp.concatenate(pieces(table), axis=1)


def take(parts, hot, mask):
    found = jnp.dot(parts, jnp.concatenate([hot] * PIECES, axis=0), preferred_element_type=F32)
    return jnp.sum(jnp.where(mask, found, 0.0), axis=0, keepdims=True)


def fold(stacked, height):
    result = stacked[:height]
    for piece in range(1, PIECES):
        result = result + stacked[piece * height : (piece + 1) * height]
    return result


def total(value):
    return jnp.sum(jnp.sum(value, axis=1, keepdims=True), axis=0, keepdims=True)


def place(scalars):
    lane = lax.broadcasted_iota(jnp.int32, (1, LO), 1)
    row = jnp.zeros((1, LO), F32)
    for index, scalar in enumerate(scalars):
        row = jnp.where(lane == index, scalar, row)
    return row


def column(row):
    size = row.shape[1]
    square = lax.broadcasted_iota(jnp.int32, (size, size), 0) == lax.broadcasted_iota(jnp.int32, (size, size), 1)
    return jnp.sum(jnp.where(square, jnp.broadcast_to(row, (size, size)), 0.0), axis=1, keepdims=True)


def flatten(square):
    lane = lax.broadcasted_iota(jnp.int32, (16, ENTRIES), 1)
    sub = lax.broadcasted_iota(jnp.int32, (16, ENTRIES), 0)
    spreader = jnp.where(lax.bitwise_and(lane, 15) == sub, 1.0, 0.0)
    wide = jnp.dot(square, spreader, precision=lax.Precision.HIGHEST, preferred_element_type=F32)
    return jnp.sum(jnp.where(lax.shift_right_logical(lane, 4) == sub, wide, 0.0), axis=0, keepdims=True)


def list_row(split_ref, curve_ref, t):
    return split_ref[0, 0, t : t + 1, :] if t < 2 else curve_ref[0, 0, t - 2 : t - 1, :]


def list_hot(hot_ref, t):
    return hot_ref[:, WIDE + t * LO : WIDE + (t + 1) * LO]


def point_hot(hot_ref, e):
    return hot_ref[:, e * POINTS : (e + 1) * POINTS]


def owner_mask():
    lane = lax.broadcasted_iota(jnp.int32, (ELEMS, ENTRIES), 1)
    return lax.bitwise_and(lane, 15) == lax.broadcasted_iota(jnp.int32, (ELEMS, ENTRIES), 0)


def coarse_line(scaled, phi_ref, pick_ref):
    acc = jnp.zeros((ELEMS, ENTRIES), F32)
    for v in range(8):
        restricted = jnp.sum(scaled * phi_ref[v : v + 1, :], axis=1, keepdims=True)
        acc = acc + restricted * pick_ref[v]
    return jnp.sum(acc, axis=0, keepdims=True)


def coarse_correction(image, phi_ref, pick_ref, xcols, xhot):
    line = take(table_parts(image), xhot, row_mask(xcols, ROWS))
    result = jnp.zeros((ELEMS, POINTS), F32)
    for v in range(8):
        vertex = jnp.sum(pick_ref[v] * line, axis=1, keepdims=True)
        result = result + vertex * phi_ref[v : v + 1, :]
    return result


def image_of(line, cols, hot):
    return fold(put(spread([line], row_mask(cols, ROWS)), hot), ROWS)


def place_in_curve():
    here = lax.axis_index("curve")
    return lax.div(here, GROUP), lax.rem(here, GROUP)


def kept_row(fits, row):
    return jnp.where(fits, row, jnp.zeros_like(row))


def write_payload(pay_ref, rows_ref, image, rows):
    inner = place_in_curve()[1]
    for g in range(GROUP):
        for r in range(8):
            pay_ref[g, 0:1, r * LO : (r + 1) * LO] = image[8 * g + r : 8 * g + r + 1, :]
        row = jnp.zeros((1, LO), F32)
        for t in range(2, LISTS):
            row = jnp.where(lax.rem(inner + WAYS[t][1] + GROUP, GROUP) == g, rows[t], row)
        pay_ref[g, 0:1, CHUNK:] = row
    rows_ref[...] = jnp.concatenate(rows[:2], axis=0)


def setup_scatter(*refs):
    sources, refs = refs[:15], refs[15:]
    slot_ref, split_ref, curve_ref, mass_ref, phi_ref, first_ref, second_ref = refs[:7]
    hot_ref, sums_ref, scale_ref, entry_ref, pick_ref, xhot_ref = refs[7:13]
    out_refs = refs[13:19]
    rhs_ref, stretch_ref, helm_ref, corner_ref, xvals_ref, xcols_ref, xcount_ref, diag_ref, sems = refs[19:]
    targets = (rhs_ref, stretch_ref, helm_ref, corner_ref, xvals_ref, xcols_ref, xcount_ref, diag_ref) + refs[:7]
    copies = [pltpu.make_async_copy(a, b, sems.at[i]) for i, (a, b) in enumerate(zip(sources, targets))]
    for copy in copies:
        copy.start()
    for copy in copies:
        copy.wait()
    columns = [column(stretch_ref[d : d + 1, :]) for d in range(3)] + [column(helm_ref[...])]
    scale_ref[...] = jnp.concatenate(columns + columns, axis=1)
    diag = columns[3] * mass_ref[...]
    for d in range(3):
        diag = diag + columns[d] * diag_ref[d : d + 1, :]
    live = lax.broadcasted_iota(jnp.int32, (16, 16), 0) < jnp.broadcast_to(xcount_ref[...], (16, 16))
    factor = flatten(jnp.where(live, xvals_ref[...], 0.0))
    cols = flatten(xcols_ref[...].astype(F32))
    entries = (cols + 0.5).astype(jnp.int32)
    entry_ref[...] = entries
    xhot_ref[...] = lane_hot(entries)
    owner = lax.bitwise_and(lax.broadcasted_iota(jnp.int32, (ELEMS, ENTRIES), 1), 15)
    corners = [column(corner_ref[v : v + 1, :].astype(F32)) for v in range(8)]
    for v in range(8):
        pick_ref[v] = jnp.where((corners[v] + 0.5).astype(jnp.int32) == owner, factor, 0.0)
    corner = jnp.concatenate(corners, axis=1)
    lists = jnp.concatenate(
        [column(list_row(split_ref, curve_ref, t).astype(F32)) for t in range(LISTS)], axis=0
    )
    lists = (lists + 0.5).astype(jnp.int32)
    acc = jnp.zeros(((1 + 2 * PIECES) * HI, LO), F32)
    weights = jnp.zeros((PIECES * ELEMS, LISTS * LO), F32)
    for e in range(ELEMS):
        slots = slot_ref[e : e + 1, :]
        hot = lane_hot(slots)
        hot_ref[:, e * POINTS : (e + 1) * POINTS] = hot
        mask = row_mask(slots, HI)
        left = spread([diag[e : e + 1, :], rhs_ref[e : e + 1, :]], mask)
        left = jnp.concatenate([jnp.where(mask, 1.0, 0.0).astype(BF16), left], axis=0)
        acc = acc + put(left, hot)
        unknown = lax.broadcasted_iota(jnp.int32, (ELEMS, 8), 0).astype(F32)
        vertex = jnp.where(jnp.abs(corner[e : e + 1, :] - unknown) < 0.5, 1.0, 0.0)
        basis = jnp.dot(vertex, phi_ref[...], precision=lax.Precision.HIGHEST, preferred_element_type=F32)
        shape = (LISTS * LO, POINTS)
        same = jnp.where(jnp.broadcast_to(slots, shape) == jnp.broadcast_to(lists, shape), 1.0, 0.0)
        weights = weights + put(jnp.concatenate(pieces(basis), axis=0), same.astype(BF16))
    weights = fold(weights, ELEMS)
    tables = []
    for field in range(3):
        first = HI + PIECES * HI * (field - 1)
        table = fold(acc[first : first + PIECES * HI], HI) if field else acc[:HI]
        sums_ref[field] = table
        tables.append(table_parts(table))
    for t in range(LISTS):
        slots = list_row(split_ref, curve_ref, t)
        hot = lane_hot(slots)
        hot_ref[:, WIDE + t * LO : WIDE + (t + 1) * LO] = hot
        mask = row_mask(slots, HI)
        rows = [take(tables[field], hot, mask) for field in range(3)]
        rows += [cols[:, :LO], cols[:, LO:], factor[:, :LO], factor[:, LO:], jnp.zeros((1, LO), F32)]
        out_refs[t][...] = jnp.concatenate(rows + [weights[:, t * LO : (t + 1) * LO]], axis=0)


def incoming_table(split_ref, curve_ref, hot_ref, rows):
    acc = jnp.zeros((PIECES * HI, LO), F32)
    for t in range(LISTS):
        mask = row_mask(list_row(split_ref, curve_ref, t), HI)
        acc = acc + put(spread([rows[t]], mask), list_hot(hot_ref, t))
    return fold(acc, HI)


def setup_gather(slot_ref, split_ref, curve_ref, hot_ref, sums_ref, phi_ref, pick_ref, entry_ref, xhot_ref, *refs):
    blocks = refs[:LISTS]
    minv_ref, dinv_ref, right_ref, nline_ref, nentry_ref, nhot_ref, weight_ref, pay_ref, rows_ref = refs[LISTS:]
    tables = [
        table_parts(
            sums_ref[field] + incoming_table(split_ref, curve_ref, hot_ref, [block[field : field + 1, :] for block in blocks])
        )
        for field in range(3)
    ]
    for e in range(ELEMS):
        mask = row_mask(slot_ref[e : e + 1, :], HI)
        hot = point_hot(hot_ref, e)
        minv_ref[e : e + 1, :] = 1.0 / take(tables[0], hot, mask)
        dinv_ref[e : e + 1, :] = 1.0 / take(tables[1], hot, mask)
        right_ref[e : e + 1, :] = take(tables[2], hot, mask)
    rows = []
    for t in range(LISTS):
        mult = take(tables[0], list_hot(hot_ref, t), row_mask(list_row(split_ref, curve_ref, t), HI))
        rows.append(jnp.where(mult > 0.5, 1.0 / jnp.where(mult > 0.5, mult, 1.0), 0.0))
        there = jnp.concatenate([blocks[t][3:4, :], blocks[t][4:5, :]], axis=1)
        weight_ref[t] = blocks[t][8:24, :]
        entries = (there + 0.5).astype(jnp.int32)
        nentry_ref[t : t + 1, :] = entries
        nhot_ref[:, t * ENTRIES : (t + 1) * ENTRIES] = lane_hot(entries)
        nline_ref[t : t + 1, :] = jnp.concatenate([blocks[t][5:6, :], blocks[t][6:7, :]], axis=1)
    line = coarse_line(right_ref[...] * minv_ref[...], phi_ref, pick_ref)
    write_payload(pay_ref, rows_ref, image_of(line, entry_ref[...], xhot_ref[...]), rows)


def operator(u, scale_ref, mass_ref, first_ref, second_ref):
    def product(parts, ref):
        rows = parts[0].shape[0]
        one = jnp.dot(jnp.concatenate(parts, axis=0), ref[0], preferred_element_type=F32)
        return one[:rows] + (one[rows:] + jnp.dot(parts[0], ref[1], preferred_element_type=F32))

    half = POINTS // 2
    parts = pieces(u)
    along = product(parts, first_ref)
    inside = product([jnp.concatenate([p[:, :half], p[:, half:]], axis=0) for p in parts], second_ref)
    second = jnp.concatenate([inside[:ELEMS, :half], inside[ELEMS:, :half]], axis=1)
    third = jnp.concatenate([inside[:ELEMS, half:], inside[ELEMS:, half:]], axis=1)
    result = scale_ref[:, 0:1] * along + scale_ref[:, 1:2] * second + scale_ref[:, 2:3] * third
    return mass_ref[...] * (result + scale_ref[:, 3:4] * u)


def scatter_points(field_ref, slot_ref, hot_ref):
    acc = jnp.zeros((PIECES * HI, LO), F32)
    for e in range(ELEMS):
        left = spread([field_ref[e : e + 1, :]], row_mask(slot_ref[e : e + 1, :], HI))
        acc = acc + put(left, point_hot(hot_ref, e))
    return fold(acc, HI)


def gather_points(table, slot_ref, hot_ref, out_ref):
    parts = table_parts(table)
    for e in range(ELEMS):
        out_ref[e : e + 1, :] = take(parts, point_hot(hot_ref, e), row_mask(slot_ref[e : e + 1, :], HI))


def send_lists(table, split_ref, curve_ref, hot_ref):
    parts = table_parts(table)
    return [
        take(parts, list_hot(hot_ref, t), row_mask(list_row(split_ref, curve_ref, t), HI)) for t in range(LISTS)
    ]


def coarse_shift(image, earlier):
    factors = []
    for other in earlier:
        size = total(other * other)
        fits = size > 1e-30
        factors.append(jnp.where(fits, total(image * other) / jnp.where(fits, size, 1.0), 0.0))
    for factor, other in zip(factors, earlier):
        image = image - factor * other
    return factors, image


def krylov_step(index, last, *refs):
    (slot_ref, split_ref, curve_ref, hot_ref, scale_ref, mass_ref, first_ref, second_ref, phi_ref, pick_ref,
     entry_ref, xhot_ref, nline_ref, nentry_ref, nhot_ref, minv_ref, dinv_ref, norm_ref, gathered_ref,
     halo_ref) = refs[:20]
    refs = refs[20:]
    image_ref, field_ref = refs[-2:]
    refs = refs[:-2]
    rows = [halo_ref[t : t + 1, :] for t in range(LISTS)]
    if index == 0:
        right_ref, plain_ref = refs[:2]
        refs = refs[2:]
        force = right_ref[...]
    else:
        weight_ref, sums_ref = refs[:2]
        refs = refs[2:]
        olds, refs = refs[: 2 * index], refs[2 * index :]
        base_refs, coarse_refs = olds[:index], olds[index:]
    base_ref, newnorm_ref, newsums_ref = refs[:3]
    refs = refs[3:]
    if index == 0:
        newweight_ref = refs[0]
        refs = refs[1:]
        for t in range(LISTS):
            newweight_ref[t] = plain_ref[t] * rows[t]
        weight_ref = newweight_ref
    else:
        force_ref = refs[0]
        refs = refs[1:]
        gather_points(
            sums_ref[...] + incoming_table(split_ref, curve_ref, hot_ref, rows), slot_ref, hot_ref, force_ref
        )
        force = force_ref[...]
    for g in range(GROUP):
        for r in range(8):
            image_ref[8 * g + r : 8 * g + r + 1, :] = gathered_ref[g, 0:1, r * LO : (r + 1) * LO]
    image = image_ref[...]
    correction = coarse_correction(image, phi_ref, pick_ref, entry_ref[...], xhot_ref[...])
    base = force * dinv_ref[...] + correction
    if index:
        factors, image = coarse_shift(image, [ref[...] for ref in coarse_refs])
        for factor, ref in zip(factors, base_refs):
            base = base - factor * ref[...]
    else:
        factors = []
    size = 1.0 + jnp.sqrt(total(image * image))
    base = base * (1.0 / size)
    base_ref[...] = base
    if not last:
        coarse_ref, *refs = refs
        coarse_ref[...] = image * (1.0 / size)
    newnorm_ref[...] = norm_ref[...]
    newnorm_ref[index : index + 1, :] = place(factors + [size])
    field_ref[...] = operator(base, scale_ref, mass_ref, first_ref, second_ref)
    table = scatter_points(field_ref, slot_ref, hot_ref)
    newsums_ref[...] = table
    rows = send_lists(table, split_ref, curve_ref, hot_ref)
    if last:
        for t in range(LISTS):
            refs[t][...] = rows[t]
        return
    pay_ref, rows_ref = refs
    gather_points(table, slot_ref, hot_ref, field_ref)
    line = coarse_line(field_ref[...] * minv_ref[...], phi_ref, pick_ref)
    image = image_of(line, entry_ref[...], xhot_ref[...])
    owner = owner_mask()
    for t in range(LISTS):
        loads = jnp.sum(weight_ref[t] * rows[t], axis=1, keepdims=True)
        line = jnp.sum(jnp.where(owner, loads, 0.0), axis=0, keepdims=True) * nline_ref[t : t + 1, :]
        image = image + image_of(line, nentry_ref[t : t + 1, :], nhot_ref[:, t * ENTRIES : (t + 1) * ENTRIES])
    write_payload(pay_ref, rows_ref, image, rows)


def sum_chunk(got_ref):
    chunk = got_ref[0, 0:1, :CHUNK]
    for g in range(1, GROUP):
        chunk = chunk + got_ref[g, 0:1, :CHUNK]
    return chunk


def after_inner(got_ref, rows_ref, pay_ref, chalo_ref):
    inner = place_in_curve()[1]
    for t in range(2, LISTS):
        there = lax.rem(inner + WAYS[t][1] + GROUP, GROUP)
        chalo_ref[t - 2 : t - 1, :] = got_ref[there, 0:1, CHUNK:]
    chunk = sum_chunk(got_ref)
    here = lax.axis_index("split")
    for g in range(GROUP):
        pay_ref[g, 0:1, :CHUNK] = chunk
        row = jnp.where(here - 1 == g, rows_ref[0:1, :], kept_row(here + 1 == g, rows_ref[1:2, :]))
        pay_ref[g, 0:1, CHUNK:] = row


def after_split(got_ref, chalo_ref, pay_ref, shalo_ref):
    here = lax.axis_index("split")
    for t in range(2):
        there = here + WAYS[t][1]
        row = got_ref[jnp.clip(there, 0, GROUP - 1), 0:1, CHUNK:]
        shalo_ref[t : t + 1, :] = kept_row(jnp.logical_and(there >= 0, there < GROUP), row)
    chunk = sum_chunk(got_ref)
    outer = place_in_curve()[0]
    up = jnp.concatenate([chalo_ref[1:2, :], chalo_ref[0:1, :]], axis=1)
    down = jnp.concatenate([chalo_ref[2:3, :], chalo_ref[3:4, :]], axis=1)
    for g in range(GROUP):
        pay_ref[g, 0:1, :CHUNK] = chunk
        pay_ref[g, 0:1, CHUNK:] = jnp.where(outer + 1 == g, up, kept_row(outer - 1 == g, down))


def after_outer(got_ref, shalo_ref, chalo_ref, pay_ref, halo_ref):
    chunk = sum_chunk(got_ref)
    for g in range(GROUP):
        pay_ref[g] = chunk
    outer, inner = place_in_curve()
    rows = [shalo_ref[t : t + 1, :] for t in range(2)]
    for t in range(2, LISTS):
        offset = WAYS[t][1]
        beyond = inner + offset >= GROUP if offset > 0 else inner + offset < 0
        there = outer + (1 if offset > 0 else -1)
        lane = CHUNK + (abs(offset) - 1) * LO
        far = got_ref[jnp.clip(there, 0, GROUP - 1), 0:1, lane : lane + LO]
        far = kept_row(jnp.logical_and(there >= 0, there < GROUP), far)
        rows.append(jnp.where(beyond, far, chalo_ref[t - 2 : t - 1, :]))
    halo_ref[...] = jnp.concatenate(rows, axis=0)


def gram(*refs):
    slot_ref, split_ref, curve_ref, hot_ref, sums_ref, minv_ref, right_ref = refs[:7]
    base_refs, force_refs = refs[7:11], refs[11:14]
    last_ref, pay_ref = refs[20:]
    rows = [ref[...] for ref in refs[14:20]]
    gather_points(
        sums_ref[...] + incoming_table(split_ref, curve_ref, hot_ref, rows), slot_ref, hot_ref, last_ref
    )
    weighted = [ref[...] * minv_ref[...] for ref in base_refs]
    scalars = []
    for ref in (right_ref, *force_refs, last_ref):
        scalars += [total(ref[...] * base) for base in weighted]
    row = place(scalars)
    for g in range(pay_ref.shape[0]):
        pay_ref[g] = row


def finish(*refs):
    got_ref, norm_ref, right_ref = refs[:3]
    base_refs, force_refs = refs[3:7], refs[7:11]
    solution_ref, residual_ref = refs[11:]
    sums = [got_ref[g] for g in range(8)]
    for g in range(8, got_ref.shape[0]):
        sums[g % 8] = sums[g % 8] + got_ref[g]
    row = ((sums[0] + sums[1]) + (sums[2] + sums[3])) + ((sums[4] + sums[5]) + (sums[6] + sums[7]))
    table = [[row[:, 4 * i + j : 4 * i + j + 1] for j in range(4)] for i in range(5)]
    relation = [[norm_ref[i : i + 1, j : j + 1] for j in range(i + 1)] for i in range(4)]

    def pair(left, right):
        acc = None
        for i, a in enumerate(left):
            inner = None
            for j, b in enumerate(right):
                if b is not None:
                    inner = b * table[i][j] if inner is None else inner + b * table[i][j]
            if a is not None and inner is not None:
                acc = a * inner if acc is None else acc + a * inner
        return acc

    def less(value, factor, other):
        if other is None:
            return value
        return -factor * other if value is None else value - factor * other

    residual = [jnp.ones((1, 1), F32)] + [None] * 4
    precond = [relation[0][0]] + [None] * 3
    direction = list(precond)
    solution = [None] * 4
    rz = pair(residual, precond)
    for k in range(ITERS):
        moved = [None] + direction
        alpha = rz / pair(moved, direction)
        solution = [less(value, -alpha, other) for value, other in zip(solution, direction)]
        residual = [less(value, alpha, other) for value, other in zip(residual, moved)]
        if k < ITERS - 1:
            shifted = [None] * 4
            for j, d in enumerate(direction[:3]):
                if d is not None:
                    for i, factor in enumerate(relation[j + 1]):
                        shifted[i] = less(shifted[i], -d, factor)
            precond = [less(value, alpha, other) for value, other in zip(precond, shifted)]
            rz_next = pair(residual, precond)
            beta = rz_next / rz
            direction = [less(value, -beta, other) for value, other in zip(precond, direction)]
            rz = rz_next
    result = solution[0] * base_refs[0][...]
    for j in range(1, 4):
        result = result + solution[j] * base_refs[j][...]
    solution_ref[...] = result
    result = right_ref[...]
    for j in range(4):
        result = result + residual[j + 1] * force_refs[j][...]
    residual_ref[...] = result


def run(body, name, args, outs, scratch=(), where=pltpu.VMEM):
    return pl.pallas_call(
        body,
        name=name,
        out_shape=[jax.ShapeDtypeStruct(shape, dtype) for shape, dtype in outs],
        in_specs=[pl.BlockSpec(memory_space=where) for _ in args],
        out_specs=[pl.BlockSpec(memory_space=pltpu.VMEM) for _ in outs],
        scratch_shapes=list(scratch),
        compiler_params=pltpu.CompilerParams(vmem_limit_bytes=VMEM_LIMIT),
    )(*args)


def shift(block, axis, offset):
    size = lax.axis_size(axis)
    route = [(i, i + offset) for i in range(size) if 0 <= i + offset < size]
    return lax.ppermute(block, axis, route)


WAYS = (("split", -1), ("split", 1), ("curve", -2), ("curve", -1), ("curve", 1), ("curve", 2))


def exchange(outgoing):
    arrived = [None] * LISTS
    for t, (axis, offset) in enumerate(WAYS):
        back = WAYS.index((axis, -offset))
        arrived[back] = shift(outgoing[t], axis, offset)
    return arrived


def reduce_image(pay, rows):
    size = lax.axis_size("curve")
    near = [list(range(first, first + GROUP)) for first in range(0, size, GROUP)]
    far = [list(range(first, size, GROUP)) for first in range(GROUP)]

    def frame(count):
        return ((GROUP, 1, CHUNK + count * LO), F32)

    got = lax.all_to_all(pay, "curve", 0, 0, axis_index_groups=near)
    pay, chalo = run(after_inner, "after_inner", (got, rows), [frame(1), ((4, LO), F32)])
    got = lax.all_to_all(pay, "split", 0, 0)
    pay, shalo = run(after_split, "after_split", (got, chalo), [frame(2), ((2, LO), F32)])
    got = lax.all_to_all(pay, "curve", 0, 0, axis_index_groups=far)
    pay, halo = run(after_outer, "after_outer", (got, shalo, chalo), [frame(0), ((LISTS, LO), F32)])
    return lax.all_to_all(pay, "curve", 0, 0, axis_index_groups=near), halo


def local(rhs_load, stretch, helm_shift, local_slot, share_curve, share_split, coarse_slot, x_vals, x_cols, x_count):
    mass, first, second, diags, coarse = element_tables()
    mass = jnp.asarray(mass.reshape(1, -1), F32)
    diags = jnp.asarray(diags, F32)
    phi = jnp.asarray(coarse, F32)
    first = jnp.asarray(table_pieces(first))
    second = jnp.asarray(table_pieces(second))
    field = ((ELEMS, POINTS), F32)
    table = ((HI, LO), F32)
    line = ((1, LO), F32)
    payload = [((GROUP, 1, CHUNK + LO), F32), ((2, LO), F32)]
    sent = [((24, LO), F32)] * LISTS
    sent_last = [line] * LISTS
    entry = jnp.int32

    sources = (rhs_load, stretch, helm_shift.reshape(1, -1), coarse_slot, x_vals, x_cols, x_count.reshape(1, -1), diags,
               local_slot, share_split, share_curve, mass, phi, first, second)
    kept = [(array.shape, array.dtype) for array in sources[8:]]
    outs = kept + [
        ((LO, WIDE + LISTS * LO), BF16), ((3, HI, LO), F32), ((ELEMS, 8), F32), ((1, ENTRIES), entry),
        ((8, ELEMS, ENTRIES), F32), ((LO, ENTRIES), BF16),
    ] + sent
    scratch = [pltpu.VMEM(array.shape, array.dtype) for array in sources[:8]]
    scratch.append(pltpu.SemaphoreType.DMA((len(sources),)))
    (local_slot, share_split, share_curve, mass, phi, first, second, hot, sums3, scale, entries, pick, xhot,
     *outgoing) = run(setup_scatter, "setup_scatter", tuple(pltpu.with_memory_space_constraint(a, pltpu.HBM) for a in sources), outs, scratch, pltpu.HBM)
    arrived = exchange(outgoing)
    shape = (local_slot, share_split, share_curve, hot)
    minv, dinv, right, nline, nentry, nhot, plain, pay, rows = run(
        setup_gather,
        "setup_gather",
        (*shape, sums3, phi, pick, entries, xhot, *arrived),
        [field, field, field, ((LISTS, ENTRIES), F32), ((LISTS, ENTRIES), entry), ((LO, LISTS * ENTRIES), BF16),
         ((LISTS, ELEMS, LO), F32)]
        + payload,
    )
    common = (*shape, scale, mass, first, second, phi, pick, entries, xhot, nline, nentry, nhot, minv, dinv)
    scratch = [pltpu.VMEM((ROWS, LO), F32), pltpu.VMEM((ELEMS, POINTS), F32)]
    norm = jnp.ones((8, LO), F32)
    bases, forces, coarses = [], [], []
    for index in range(ITERS):
        last = index == ITERS - 1
        gathered, halo = reduce_image(pay, rows)
        own = (right, plain) if index == 0 else (weight, sums, *bases, *coarses)
        outs = [field, ((8, LO), F32), table] + [((LISTS, ELEMS, LO), F32) if index == 0 else field]
        outs += [] if last else [((ROWS, LO), F32)]
        base, norm, sums, extra, *rest = run(
            functools.partial(krylov_step, index, last),
            f"krylov_step{index}",
            (*common, norm, gathered, halo, *own),
            outs + (sent_last if last else payload),
            scratch,
        )
        bases.append(base)
        if index == 0:
            weight = extra
        else:
            forces.append(extra)
        if not last:
            coarse, pay, rows = rest
            coarses.append(coarse)
    devices = lax.axis_size("curve") * lax.axis_size("split")
    force, pay = run(
        gram,
        "gram",
        (*shape, sums, minv, right, *bases, *forces, *exchange(rest)),
        [field, ((devices, 1, LO), F32)],
    )
    got = lax.all_to_all(pay, ("curve", "split"), 0, 0)
    solution, residual = run(
        finish, "finish", (got, norm, right, *bases, *forces, force), [field, field]
    )
    return solution, residual


def solution(mesh):
    in_specs = (
        P(("curve", "split"), None),
        P(None, ("curve", "split")),
        P(("curve", "split")),
        P(("curve", "split"), None),
        P("curve", "split", None, None),
        P("curve", "split", None, None),
        P(None, ("curve", "split")),
        P(None, ("curve", "split")),
        P(None, ("curve", "split")),
        P(("curve", "split")),
    )
    out_specs = (P(("curve", "split"), None), P(("curve", "split"), None))
    return jax.shard_map(local, mesh=mesh, in_specs=in_specs, out_specs=out_specs, check_vma=False)
```

```python
import functools

import jax
import jax.numpy as jnp
import ml_dtypes
import numpy as np
from jax import lax
from jax.experimental import pallas as pl
from jax.experimental.pallas import tpu as pltpu
from jax.sharding import PartitionSpec as P

ITERS = 4
HI = 48
LO = 128
ELEMS = 16
POINTS = 512
LISTS = 6
WIDE = ELEMS * POINTS
ENTRIES = 256
ROWS = 64
GROUP = 8
CHUNK = ROWS * LO // GROUP
PIECES = 2
LATE = 13
F32 = jnp.float32
BF16 = jnp.bfloat16
VMEM_LIMIT = 16 << 20


def element_tables():
    poly_order = 7
    node_count = poly_order + 1
    nodes = -np.cos(np.pi * np.arange(node_count) / poly_order)
    legendre = np.zeros((node_count, node_count))

    def fill():
        legendre[:, 0] = 1.0
        legendre[:, 1] = nodes
        for degree in range(2, node_count):
            legendre[:, degree] = (
                (2 * degree - 1) * nodes * legendre[:, degree - 1] - (degree - 1) * legendre[:, degree - 2]
            ) / degree

    for _ in range(60):
        fill()
        nodes = nodes - (nodes * legendre[:, poly_order] - legendre[:, poly_order - 1]) / (
            node_count * legendre[:, poly_order]
        )
    fill()
    top = legendre[:, poly_order]
    weights = 2.0 / (poly_order * node_count * top * top)
    deriv = np.zeros((node_count, node_count))
    for i in range(node_count):
        for j in range(node_count):
            if i != j:
                deriv[i, j] = top[i] / (top[j] * (nodes[i] - nodes[j]))
    deriv[0, 0] = -poly_order * node_count / 4.0
    deriv[poly_order, poly_order] = poly_order * node_count / 4.0
    mass = (weights[:, None, None] * weights[None, :, None] * weights[None, None, :]).reshape(-1)
    line = deriv.T @ (weights[:, None] * deriv)
    scaled = line / weights[None, :]
    eye = np.eye(node_count)
    first = np.kron(scaled, np.eye(64))
    second = np.kron(np.eye(4), np.kron(scaled, eye))
    third = np.kron(np.eye(4), np.kron(eye, scaled))
    diag = np.diag(scaled)
    ones = np.ones(node_count)
    diags = np.stack(
        [
            mass * np.kron(diag, np.kron(ones, ones)),
            mass * np.kron(ones, np.kron(diag, ones)),
            mass * np.kron(ones, np.kron(ones, diag)),
        ]
    )
    hats = np.stack([(1.0 - nodes) / 2.0, (1.0 + nodes) / 2.0])
    coarse = (
        hats[:, None, None, :, None, None]
        * hats[None, :, None, None, :, None]
        * hats[None, None, :, None, None, :]
    ).reshape(8, -1)
    return mass, first, np.concatenate([second, third], axis=1), diags, coarse


def table_pieces(table):
    rest = np.asarray(table, np.float32)
    pieces = []
    for _ in range(PIECES):
        piece = rest.astype(ml_dtypes.bfloat16)
        pieces.append(piece)
        rest = rest - piece.astype(np.float32)
    return np.stack(pieces)


def pieces(value):
    found = []
    for left in reversed(range(PIECES)):
        found.append(value.astype(BF16))
        if left:
            value = value - found[-1].astype(F32)
    return found


def row_mask(slots, height):
    high = lax.shift_right_logical(slots, 7)
    width = slots.shape[1]
    return jnp.broadcast_to(high, (height, width)) == lax.broadcasted_iota(jnp.int32, (height, width), 0)


def lane_hot(slots):
    low = lax.bitwise_and(slots, LO - 1)
    width = slots.shape[1]
    hot = jnp.broadcast_to(low, (LO, width)) == lax.broadcasted_iota(jnp.int32, (LO, width), 0)
    return jnp.where(hot, 1.0, 0.0).astype(BF16)


def spread(values, mask):
    wide = [jnp.where(mask, jnp.broadcast_to(value, mask.shape), 0.0) for value in values]
    return jnp.concatenate([piece for value in wide for piece in pieces(value)], axis=0)


def put(left, hot):
    return lax.dot_general(left, hot, (((1,), (1,)), ((), ())), preferred_element_type=F32)


def table_parts(table):
    return jnp.concatenate(pieces(table), axis=1)


def take(parts, hot, mask):
    found = jnp.dot(parts, jnp.concatenate([hot] * PIECES, axis=0), preferred_element_type=F32)
    return jnp.sum(jnp.where(mask, found, 0.0), axis=0, keepdims=True)


def fold(stacked, height):
    result = stacked[:height]
    for piece in range(1, PIECES):
        result = result + stacked[piece * height : (piece + 1) * height]
    return result


def total(value):
    return jnp.sum(jnp.sum(value, axis=1, keepdims=True), axis=0, keepdims=True)


def place(scalars):
    lane = lax.broadcasted_iota(jnp.int32, (1, LO), 1)
    row = jnp.zeros((1, LO), F32)
    for index, scalar in enumerate(scalars):
        row = jnp.where(lane == index, scalar, row)
    return row


def column(row):
    size = row.shape[1]
    square = lax.broadcasted_iota(jnp.int32, (size, size), 0) == lax.broadcasted_iota(jnp.int32, (size, size), 1)
    return jnp.sum(jnp.where(square, jnp.broadcast_to(row, (size, size)), 0.0), axis=1, keepdims=True)


def flatten(square):
    lane = lax.broadcasted_iota(jnp.int32, (16, ENTRIES), 1)
    sub = lax.broadcasted_iota(jnp.int32, (16, ENTRIES), 0)
    spreader = jnp.where(lax.bitwise_and(lane, 15) == sub, 1.0, 0.0)
    wide = jnp.dot(square, spreader, precision=lax.Precision.HIGHEST, preferred_element_type=F32)
    return jnp.sum(jnp.where(lax.shift_right_logical(lane, 4) == sub, wide, 0.0), axis=0, keepdims=True)


def list_row(split_ref, curve_ref, t):
    return split_ref[0, 0, t : t + 1, :] if t < 2 else curve_ref[0, 0, t - 2 : t - 1, :]


def list_mask(split_ref, curve_ref):
    rows = [list_row(split_ref, curve_ref, t) for t in range(LISTS)]
    return row_mask(jnp.concatenate(rows, axis=1), HI)


def by_list(wide):
    return [wide[:, t * LO : (t + 1) * LO] for t in range(LISTS)]


def point_hot(hot_ref, e):
    return hot_ref[:, e * POINTS : (e + 1) * POINTS]


def owner_mask():
    lane = lax.broadcasted_iota(jnp.int32, (ELEMS, ENTRIES), 1)
    return lax.bitwise_and(lane, 15) == lax.broadcasted_iota(jnp.int32, (ELEMS, ENTRIES), 0)


def coarse_line(scaled, phi_ref, pick_ref):
    acc = jnp.zeros((ELEMS, ENTRIES), F32)
    for v in range(8):
        restricted = jnp.sum(scaled * phi_ref[v : v + 1, :], axis=1, keepdims=True)
        acc = acc + restricted * pick_ref[v]
    return jnp.sum(acc, axis=0, keepdims=True)


def coarse_correction(image, phi_ref, pick_ref, xcols, xhot):
    line = take(table_parts(image), xhot, row_mask(xcols, ROWS))
    result = jnp.zeros((ELEMS, POINTS), F32)
    for v in range(8):
        vertex = jnp.sum(pick_ref[v] * line, axis=1, keepdims=True)
        result = result + vertex * phi_ref[v : v + 1, :]
    return result


def image_of(line, cols, hot):
    return fold(put(spread([line], row_mask(cols, ROWS)), hot), ROWS)


def place_in_curve():
    here = lax.axis_index("curve")
    return lax.div(here, GROUP), lax.rem(here, GROUP)


def kept_row(fits, row):
    return jnp.where(fits, row, jnp.zeros_like(row))


def write_payload(pay_ref, rows_ref, image, rows):
    inner = place_in_curve()[1]
    for g in range(GROUP):
        for r in range(8):
            pay_ref[g, 0:1, r * LO : (r + 1) * LO] = image[8 * g + r : 8 * g + r + 1, :]
        row = jnp.zeros((1, LO), F32)
        for t in range(2, LISTS):
            row = jnp.where(lax.rem(inner + WAYS[t][1] + GROUP, GROUP) == g, rows[t], row)
        pay_ref[g, 0:1, CHUNK:] = row
    rows_ref[...] = jnp.concatenate(rows[:2], axis=0)


def setup_scatter(*refs):
    sources, refs = refs[:15], refs[15:]
    slot_ref, split_ref, curve_ref, mass_ref, phi_ref, first_ref, second_ref = refs[:7]
    hot_ref, sums_ref, scale_ref, entry_ref, pick_ref, xhot_ref = refs[7:13]
    out_refs = refs[13:19]
    rhs_ref, stretch_ref, helm_ref, corner_ref, xvals_ref, xcols_ref, xcount_ref, diag_ref, sems = refs[19:]
    targets = (rhs_ref, stretch_ref, helm_ref, corner_ref, xvals_ref, xcols_ref, xcount_ref, diag_ref) + refs[:7]
    copies = [pltpu.make_async_copy(a, b, sems.at[i]) for i, (a, b) in enumerate(zip(sources, targets))]
    for copy in copies:
        copy.start()
    for copy in copies[:LATE]:
        copy.wait()
    columns = [column(stretch_ref[d : d + 1, :]) for d in range(3)] + [column(helm_ref[...])]
    scale_ref[...] = jnp.concatenate(columns + columns, axis=1)
    diag = columns[3] * mass_ref[...]
    for d in range(3):
        diag = diag + columns[d] * diag_ref[d : d + 1, :]
    live = lax.broadcasted_iota(jnp.int32, (16, 16), 0) < jnp.broadcast_to(xcount_ref[...], (16, 16))
    factor = flatten(jnp.where(live, xvals_ref[...], 0.0))
    cols = flatten(xcols_ref[...].astype(F32))
    entries = (cols + 0.5).astype(jnp.int32)
    entry_ref[...] = entries
    xhot_ref[...] = lane_hot(entries)
    owner = lax.bitwise_and(lax.broadcasted_iota(jnp.int32, (ELEMS, ENTRIES), 1), 15)
    corners = [column(corner_ref[v : v + 1, :].astype(F32)) for v in range(8)]
    for v in range(8):
        pick_ref[v] = jnp.where((corners[v] + 0.5).astype(jnp.int32) == owner, factor, 0.0)
    corner = jnp.concatenate(corners, axis=1)
    lists = jnp.concatenate(
        [column(list_row(split_ref, curve_ref, t).astype(F32)) for t in range(LISTS)], axis=0
    )
    lists = (lists + 0.5).astype(jnp.int32)
    acc = jnp.zeros(((1 + 2 * PIECES) * HI, LO), F32)
    weights = jnp.zeros((PIECES * ELEMS, LISTS * LO), F32)
    for e in range(ELEMS):
        slots = slot_ref[e : e + 1, :]
        hot = lane_hot(slots)
        hot_ref[:, e * POINTS : (e + 1) * POINTS] = hot
        mask = row_mask(slots, HI)
        left = spread([diag[e : e + 1, :], rhs_ref[e : e + 1, :]], mask)
        left = jnp.concatenate([jnp.where(mask, 1.0, 0.0).astype(BF16), left], axis=0)
        acc = acc + put(left, hot)
        unknown = lax.broadcasted_iota(jnp.int32, (ELEMS, 8), 0).astype(F32)
        vertex = jnp.where(jnp.abs(corner[e : e + 1, :] - unknown) < 0.5, 1.0, 0.0)
        basis = jnp.dot(vertex, phi_ref[...], precision=lax.Precision.HIGHEST, preferred_element_type=F32)
        shape = (LISTS * LO, POINTS)
        same = jnp.where(jnp.broadcast_to(slots, shape) == jnp.broadcast_to(lists, shape), 1.0, 0.0)
        weights = weights + put(jnp.concatenate(pieces(basis), axis=0), same.astype(BF16))
    weights = fold(weights, ELEMS)
    tables = []
    for field in range(3):
        first = HI + PIECES * HI * (field - 1)
        table = fold(acc[first : first + PIECES * HI], HI) if field else acc[:HI]
        sums_ref[field] = table
        tables.append(table_parts(table))
    slots = jnp.concatenate([list_row(split_ref, curve_ref, t) for t in range(LISTS)], axis=1)
    hot = lane_hot(slots)
    hot_ref[:, WIDE:] = hot
    mask = row_mask(slots, HI)
    rows = [take(tables[field], hot, mask) for field in range(3)]
    plain = [cols[:, :LO], cols[:, LO:], factor[:, :LO], factor[:, LO:], jnp.zeros((1, LO), F32)]
    for t in range(LISTS):
        lanes = slice(t * LO, (t + 1) * LO)
        out_refs[t][...] = jnp.concatenate([row[:, lanes] for row in rows] + plain + [weights[:, lanes]], axis=0)
    for copy in copies[LATE:]:
        copy.wait()


def incoming_table(split_ref, curve_ref, hot_ref, rows):
    left = spread([jnp.concatenate(rows, axis=1)], list_mask(split_ref, curve_ref))
    return fold(put(left, hot_ref[:, WIDE:]), HI)


def setup_gather(slot_ref, split_ref, curve_ref, hot_ref, sums_ref, phi_ref, pick_ref, entry_ref, xhot_ref, *refs):
    blocks = refs[:LISTS]
    minv_ref, dinv_ref, right_ref, nline_ref, nentry_ref, nhot_ref, weight_ref, pay_ref, rows_ref = refs[LISTS:]
    tables = [
        table_parts(
            sums_ref[field] + incoming_table(split_ref, curve_ref, hot_ref, [block[field : field + 1, :] for block in blocks])
        )
        for field in range(3)
    ]
    for e in range(ELEMS):
        mask = row_mask(slot_ref[e : e + 1, :], HI)
        hot = point_hot(hot_ref, e)
        minv_ref[e : e + 1, :] = 1.0 / take(tables[0], hot, mask)
        dinv_ref[e : e + 1, :] = 1.0 / take(tables[1], hot, mask)
        right_ref[e : e + 1, :] = take(tables[2], hot, mask)
    mult = take(tables[0], hot_ref[:, WIDE:], list_mask(split_ref, curve_ref))
    rows = by_list(jnp.where(mult > 0.5, 1.0 / jnp.where(mult > 0.5, mult, 1.0), 0.0))
    own = entry_ref[...]
    nentry_ref[:, :ENTRIES] = own
    nhot_ref[:, :ENTRIES] = xhot_ref[...]
    for t in range(LISTS):
        there = jnp.concatenate([blocks[t][3:4, :], blocks[t][4:5, :]], axis=1)
        weight_ref[t] = blocks[t][8:24, :]
        entries = (there + 0.5).astype(jnp.int32)
        lanes = slice((t + 1) * ENTRIES, (t + 2) * ENTRIES)
        nentry_ref[:, lanes] = entries
        nhot_ref[:, lanes] = lane_hot(entries)
        nline_ref[t : t + 1, :] = jnp.concatenate([blocks[t][5:6, :], blocks[t][6:7, :]], axis=1)
    line = coarse_line(right_ref[...] * minv_ref[...], phi_ref, pick_ref)
    write_payload(pay_ref, rows_ref, image_of(line, entry_ref[...], xhot_ref[...]), rows)


def operator(u, scale_ref, mass_ref, first_ref, second_ref):
    def product(parts, ref):
        rows = parts[0].shape[0]
        one = jnp.dot(jnp.concatenate(parts, axis=0), ref[0], preferred_element_type=F32)
        return one[:rows] + (one[rows:] + jnp.dot(parts[0], ref[1], preferred_element_type=F32))

    half = POINTS // 2
    parts = pieces(u)
    along = product(parts, first_ref)
    inside = product([jnp.concatenate([p[:, :half], p[:, half:]], axis=0) for p in parts], second_ref)
    second = jnp.concatenate([inside[:ELEMS, :half], inside[ELEMS:, :half]], axis=1)
    third = jnp.concatenate([inside[:ELEMS, half:], inside[ELEMS:, half:]], axis=1)
    result = scale_ref[:, 0:1] * along + scale_ref[:, 1:2] * second + scale_ref[:, 2:3] * third
    return mass_ref[...] * (result + scale_ref[:, 3:4] * u)


def scatter_points(field_ref, slot_ref, hot_ref):
    acc = jnp.zeros((PIECES * HI, LO), F32)
    for e in range(ELEMS):
        left = spread([field_ref[e : e + 1, :]], row_mask(slot_ref[e : e + 1, :], HI))
        acc = acc + put(left, point_hot(hot_ref, e))
    return fold(acc, HI)


def gather_points(table, slot_ref, hot_ref, out_ref):
    parts = table_parts(table)
    for e in range(ELEMS):
        out_ref[e : e + 1, :] = take(parts, point_hot(hot_ref, e), row_mask(slot_ref[e : e + 1, :], HI))


def send_lists(table, split_ref, curve_ref, hot_ref):
    return by_list(take(table_parts(table), hot_ref[:, WIDE:], list_mask(split_ref, curve_ref)))


def coarse_shift(image, earlier):
    factors = []
    for other in earlier:
        size = total(other * other)
        fits = size > 1e-30
        factors.append(jnp.where(fits, total(image * other) / jnp.where(fits, size, 1.0), 0.0))
    for factor, other in zip(factors, earlier):
        image = image - factor * other
    return factors, image


def krylov_step(index, last, *refs):
    (slot_ref, split_ref, curve_ref, hot_ref, scale_ref, mass_ref, first_ref, second_ref, phi_ref, pick_ref,
     entry_ref, xhot_ref, nline_ref, nentry_ref, nhot_ref, minv_ref, dinv_ref, norm_ref, gathered_ref,
     halo_ref) = refs[:20]
    refs = refs[20:]
    image_ref, field_ref = refs[-2:]
    refs = refs[:-2]
    rows = [halo_ref[t : t + 1, :] for t in range(LISTS)]
    if index == 0:
        right_ref, plain_ref = refs[:2]
        refs = refs[2:]
        force = right_ref[...]
    else:
        weight_ref, sums_ref = refs[:2]
        refs = refs[2:]
        olds, refs = refs[: 2 * index], refs[2 * index :]
        base_refs, coarse_refs = olds[:index], olds[index:]
    base_ref, newnorm_ref, newsums_ref = refs[:3]
    refs = refs[3:]
    if index == 0:
        newweight_ref = refs[0]
        refs = refs[1:]
        for t in range(LISTS):
            newweight_ref[t] = plain_ref[t] * rows[t]
        weight_ref = newweight_ref
    else:
        force_ref = refs[0]
        refs = refs[1:]
        gather_points(
            sums_ref[...] + incoming_table(split_ref, curve_ref, hot_ref, rows), slot_ref, hot_ref, force_ref
        )
        force = force_ref[...]
    for g in range(GROUP):
        for r in range(8):
            image_ref[8 * g + r : 8 * g + r + 1, :] = gathered_ref[g, 0:1, r * LO : (r + 1) * LO]
    image = image_ref[...]
    correction = coarse_correction(image, phi_ref, pick_ref, entry_ref[...], xhot_ref[...])
    base = force * dinv_ref[...] + correction
    if index:
        factors, image = coarse_shift(image, [ref[...] for ref in coarse_refs])
        for factor, ref in zip(factors, base_refs):
            base = base - factor * ref[...]
    else:
        factors = []
    size = 1.0 + jnp.sqrt(total(image * image))
    base = base * (1.0 / size)
    base_ref[...] = base
    if not last:
        coarse_ref, *refs = refs
        coarse_ref[...] = image * (1.0 / size)
    newnorm_ref[...] = norm_ref[...]
    newnorm_ref[index : index + 1, :] = place(factors + [size])
    field_ref[...] = operator(base, scale_ref, mass_ref, first_ref, second_ref)
    table = scatter_points(field_ref, slot_ref, hot_ref)
    newsums_ref[...] = table
    rows = send_lists(table, split_ref, curve_ref, hot_ref)
    if last:
        for t in range(LISTS):
            refs[t][...] = rows[t]
        return
    pay_ref, rows_ref = refs
    gather_points(table, slot_ref, hot_ref, field_ref)
    line = coarse_line(field_ref[...] * minv_ref[...], phi_ref, pick_ref)
    lines = [line]
    owner = owner_mask()
    for t in range(LISTS):
        loads = jnp.sum(weight_ref[t] * rows[t], axis=1, keepdims=True)
        lines.append(jnp.sum(jnp.where(owner, loads, 0.0), axis=0, keepdims=True) * nline_ref[t : t + 1, :])
    image = image_of(jnp.concatenate(lines, axis=1), nentry_ref[...], nhot_ref[...])
    write_payload(pay_ref, rows_ref, image, rows)


def sum_chunk(got_ref):
    chunk = got_ref[0, 0:1, :CHUNK]
    for g in range(1, GROUP):
        chunk = chunk + got_ref[g, 0:1, :CHUNK]
    return chunk


def after_inner(got_ref, rows_ref, pay_ref, chalo_ref):
    inner = place_in_curve()[1]
    for t in range(2, LISTS):
        there = lax.rem(inner + WAYS[t][1] + GROUP, GROUP)
        chalo_ref[t - 2 : t - 1, :] = got_ref[there, 0:1, CHUNK:]
    chunk = sum_chunk(got_ref)
    here = lax.axis_index("split")
    for g in range(GROUP):
        pay_ref[g, 0:1, :CHUNK] = chunk
        row = jnp.where(here - 1 == g, rows_ref[0:1, :], kept_row(here + 1 == g, rows_ref[1:2, :]))
        pay_ref[g, 0:1, CHUNK:] = row


def after_split(got_ref, chalo_ref, pay_ref, shalo_ref):
    here = lax.axis_index("split")
    for t in range(2):
        there = here + WAYS[t][1]
        row = got_ref[jnp.clip(there, 0, GROUP - 1), 0:1, CHUNK:]
        shalo_ref[t : t + 1, :] = kept_row(jnp.logical_and(there >= 0, there < GROUP), row)
    chunk = sum_chunk(got_ref)
    outer = place_in_curve()[0]
    up = jnp.concatenate([chalo_ref[1:2, :], chalo_ref[0:1, :]], axis=1)
    down = jnp.concatenate([chalo_ref[2:3, :], chalo_ref[3:4, :]], axis=1)
    for g in range(GROUP):
        pay_ref[g, 0:1, :CHUNK] = chunk
        pay_ref[g, 0:1, CHUNK:] = jnp.where(outer + 1 == g, up, kept_row(outer - 1 == g, down))


def after_outer(got_ref, shalo_ref, chalo_ref, pay_ref, halo_ref):
    chunk = sum_chunk(got_ref)
    for g in range(GROUP):
        pay_ref[g] = chunk
    outer, inner = place_in_curve()
    rows = [shalo_ref[t : t + 1, :] for t in range(2)]
    for t in range(2, LISTS):
        offset = WAYS[t][1]
        beyond = inner + offset >= GROUP if offset > 0 else inner + offset < 0
        there = outer + (1 if offset > 0 else -1)
        lane = CHUNK + (abs(offset) - 1) * LO
        far = got_ref[jnp.clip(there, 0, GROUP - 1), 0:1, lane : lane + LO]
        far = kept_row(jnp.logical_and(there >= 0, there < GROUP), far)
        rows.append(jnp.where(beyond, far, chalo_ref[t - 2 : t - 1, :]))
    halo_ref[...] = jnp.concatenate(rows, axis=0)


def gram(*refs):
    slot_ref, split_ref, curve_ref, hot_ref, sums_ref, minv_ref, right_ref = refs[:7]
    base_refs, force_refs = refs[7:11], refs[11:14]
    last_ref, pay_ref = refs[20:]
    rows = [ref[...] for ref in refs[14:20]]
    gather_points(
        sums_ref[...] + incoming_table(split_ref, curve_ref, hot_ref, rows), slot_ref, hot_ref, last_ref
    )
    weighted = [ref[...] * minv_ref[...] for ref in base_refs]
    scalars = []
    for ref in (right_ref, *force_refs, last_ref):
        scalars += [total(ref[...] * base) for base in weighted]
    row = place(scalars)
    for g in range(pay_ref.shape[0]):
        pay_ref[g] = row


def finish(*refs):
    got_ref, norm_ref, right_ref = refs[:3]
    base_refs, force_refs = refs[3:7], refs[7:11]
    solution_ref, residual_ref = refs[11:]
    sums = [got_ref[g] for g in range(8)]
    for g in range(8, got_ref.shape[0]):
        sums[g % 8] = sums[g % 8] + got_ref[g]
    row = ((sums[0] + sums[1]) + (sums[2] + sums[3])) + ((sums[4] + sums[5]) + (sums[6] + sums[7]))
    table = [[row[:, 4 * i + j : 4 * i + j + 1] for j in range(4)] for i in range(5)]
    relation = [[norm_ref[i : i + 1, j : j + 1] for j in range(i + 1)] for i in range(4)]

    def pair(left, right):
        acc = None
        for i, a in enumerate(left):
            inner = None
            for j, b in enumerate(right):
                if b is not None:
                    inner = b * table[i][j] if inner is None else inner + b * table[i][j]
            if a is not None and inner is not None:
                acc = a * inner if acc is None else acc + a * inner
        return acc

    def less(value, factor, other):
        if other is None:
            return value
        return -factor * other if value is None else value - factor * other

    residual = [jnp.ones((1, 1), F32)] + [None] * 4
    precond = [relation[0][0]] + [None] * 3
    direction = list(precond)
    solution = [None] * 4
    rz = pair(residual, precond)
    for k in range(ITERS):
        moved = [None] + direction
        alpha = rz / pair(moved, direction)
        solution = [less(value, -alpha, other) for value, other in zip(solution, direction)]
        residual = [less(value, alpha, other) for value, other in zip(residual, moved)]
        if k < ITERS - 1:
            shifted = [None] * 4
            for j, d in enumerate(direction[:3]):
                if d is not None:
                    for i, factor in enumerate(relation[j + 1]):
                        shifted[i] = less(shifted[i], -d, factor)
            precond = [less(value, alpha, other) for value, other in zip(precond, shifted)]
            rz_next = pair(residual, precond)
            beta = rz_next / rz
            direction = [less(value, -beta, other) for value, other in zip(precond, direction)]
            rz = rz_next
    result = solution[0] * base_refs[0][...]
    for j in range(1, 4):
        result = result + solution[j] * base_refs[j][...]
    solution_ref[...] = result
    result = right_ref[...]
    for j in range(4):
        result = result + residual[j + 1] * force_refs[j][...]
    residual_ref[...] = result


def run(body, name, args, outs, scratch=(), where=pltpu.VMEM):
    return pl.pallas_call(
        body,
        name=name,
        out_shape=[jax.ShapeDtypeStruct(shape, dtype) for shape, dtype in outs],
        in_specs=[pl.BlockSpec(memory_space=where) for _ in args],
        out_specs=[pl.BlockSpec(memory_space=pltpu.VMEM) for _ in outs],
        scratch_shapes=list(scratch),
        compiler_params=pltpu.CompilerParams(vmem_limit_bytes=VMEM_LIMIT),
    )(*args)


def shift(block, axis, offset):
    size = lax.axis_size(axis)
    route = [(i, i + offset) for i in range(size) if 0 <= i + offset < size]
    return lax.ppermute(block, axis, route)


WAYS = (("split", -1), ("split", 1), ("curve", -2), ("curve", -1), ("curve", 1), ("curve", 2))


def exchange(outgoing):
    arrived = [None] * LISTS
    for t, (axis, offset) in enumerate(WAYS):
        back = WAYS.index((axis, -offset))
        arrived[back] = shift(outgoing[t], axis, offset)
    return arrived


def reduce_image(pay, rows):
    size = lax.axis_size("curve")
    near = [list(range(first, first + GROUP)) for first in range(0, size, GROUP)]
    far = [list(range(first, size, GROUP)) for first in range(GROUP)]

    def frame(count):
        return ((GROUP, 1, CHUNK + count * LO), F32)

    got = lax.all_to_all(pay, "curve", 0, 0, axis_index_groups=near)
    pay, chalo = run(after_inner, "after_inner", (got, rows), [frame(1), ((4, LO), F32)])
    got = lax.all_to_all(pay, "split", 0, 0)
    pay, shalo = run(after_split, "after_split", (got, chalo), [frame(2), ((2, LO), F32)])
    got = lax.all_to_all(pay, "curve", 0, 0, axis_index_groups=far)
    pay, halo = run(after_outer, "after_outer", (got, shalo, chalo), [frame(0), ((LISTS, LO), F32)])
    return lax.all_to_all(pay, "curve", 0, 0, axis_index_groups=near), halo


def local(rhs_load, stretch, helm_shift, local_slot, share_curve, share_split, coarse_slot, x_vals, x_cols, x_count):
    mass, first, second, diags, coarse = element_tables()
    mass = jnp.asarray(mass.reshape(1, -1), F32)
    diags = jnp.asarray(diags, F32)
    phi = jnp.asarray(coarse, F32)
    first = jnp.asarray(table_pieces(first))
    second = jnp.asarray(table_pieces(second))
    field = ((ELEMS, POINTS), F32)
    table = ((HI, LO), F32)
    line = ((1, LO), F32)
    payload = [((GROUP, 1, CHUNK + LO), F32), ((2, LO), F32)]
    sent = [((24, LO), F32)] * LISTS
    sent_last = [line] * LISTS
    entry = jnp.int32

    sources = (rhs_load, stretch, helm_shift.reshape(1, -1), coarse_slot, x_vals, x_cols, x_count.reshape(1, -1), diags,
               local_slot, share_split, share_curve, mass, phi, first, second)
    kept = [(array.shape, array.dtype) for array in sources[8:]]
    outs = kept + [
        ((LO, WIDE + LISTS * LO), BF16), ((3, HI, LO), F32), ((ELEMS, 8), F32), ((1, ENTRIES), entry),
        ((8, ELEMS, ENTRIES), F32), ((LO, ENTRIES), BF16),
    ] + sent
    scratch = [pltpu.VMEM(array.shape, array.dtype) for array in sources[:8]]
    scratch.append(pltpu.SemaphoreType.DMA((len(sources),)))
    (local_slot, share_split, share_curve, mass, phi, first, second, hot, sums3, scale, entries, pick, xhot,
     *outgoing) = run(setup_scatter, "setup_scatter", tuple(pltpu.with_memory_space_constraint(a, pltpu.HBM) for a in sources), outs, scratch, pltpu.HBM)
    arrived = exchange(outgoing)
    shape = (local_slot, share_split, share_curve, hot)
    minv, dinv, right, nline, nentry, nhot, plain, pay, rows = run(
        setup_gather,
        "setup_gather",
        (*shape, sums3, phi, pick, entries, xhot, *arrived),
        [field, field, field, ((LISTS, ENTRIES), F32), ((1, (LISTS + 1) * ENTRIES), entry), ((LO, (LISTS + 1) * ENTRIES), BF16),
         ((LISTS, ELEMS, LO), F32)]
        + payload,
    )
    common = (*shape, scale, mass, first, second, phi, pick, entries, xhot, nline, nentry, nhot, minv, dinv)
    scratch = [pltpu.VMEM((ROWS, LO), F32), pltpu.VMEM((ELEMS, POINTS), F32)]
    norm = jnp.ones((8, LO), F32)
    bases, forces, coarses = [], [], []
    for index in range(ITERS):
        last = index == ITERS - 1
        gathered, halo = reduce_image(pay, rows)
        own = (right, plain) if index == 0 else (weight, sums, *bases, *coarses)
        outs = [field, ((8, LO), F32), table] + [((LISTS, ELEMS, LO), F32) if index == 0 else field]
        outs += [] if last else [((ROWS, LO), F32)]
        base, norm, sums, extra, *rest = run(
            functools.partial(krylov_step, index, last),
            f"krylov_step{index}",
            (*common, norm, gathered, halo, *own),
            outs + (sent_last if last else payload),
            scratch,
        )
        bases.append(base)
        if index == 0:
            weight = extra
        else:
            forces.append(extra)
        if not last:
            coarse, pay, rows = rest
            coarses.append(coarse)
    devices = lax.axis_size("curve") * lax.axis_size("split")
    force, pay = run(
        gram,
        "gram",
        (*shape, sums, minv, right, *bases, *forces, *exchange(rest)),
        [field, ((devices, 1, LO), F32)],
    )
    got = lax.all_to_all(pay, ("curve", "split"), 0, 0)
    solution, residual = run(
        finish, "finish", (got, norm, right, *bases, *forces, force), [field, field]
    )
    return solution, residual


def solution(mesh):
    in_specs = (
        P(("curve", "split"), None),
        P(None, ("curve", "split")),
        P(("curve", "split")),
        P(("curve", "split"), None),
        P("curve", "split", None, None),
        P("curve", "split", None, None),
        P(None, ("curve", "split")),
        P(None, ("curve", "split")),
        P(None, ("curve", "split")),
        P(("curve", "split")),
    )
    out_specs = (P(("curve", "split"), None), P(("curve", "split"), None))
    return jax.shard_map(local, mesh=mesh, in_specs=in_specs, out_specs=out_specs, check_vma=False)
```

```python
import functools

import jax
import jax.numpy as jnp
import ml_dtypes
import numpy as np
from jax import lax
from jax.experimental import pallas as pl
from jax.experimental.pallas import tpu as pltpu
from jax.sharding import PartitionSpec as P

ITERS = 4
HI = 48
LO = 128
ELEMS = 16
POINTS = 512
LISTS = 6
WIDE = ELEMS * POINTS
ENTRIES = 256
ROWS = 64
GROUP = 8
CHUNK = ROWS * LO // GROUP
PIECES = 3
LATE = 13
F32 = jnp.float32
BF16 = jnp.bfloat16
VMEM_LIMIT = 16 << 20


def element_tables():
    poly_order = 7
    node_count = poly_order + 1
    nodes = -np.cos(np.pi * np.arange(node_count) / poly_order)
    legendre = np.zeros((node_count, node_count))

    def fill():
        legendre[:, 0] = 1.0
        legendre[:, 1] = nodes
        for degree in range(2, node_count):
            legendre[:, degree] = (
                (2 * degree - 1) * nodes * legendre[:, degree - 1] - (degree - 1) * legendre[:, degree - 2]
            ) / degree

    for _ in range(60):
        fill()
        nodes = nodes - (nodes * legendre[:, poly_order] - legendre[:, poly_order - 1]) / (
            node_count * legendre[:, poly_order]
        )
    fill()
    top = legendre[:, poly_order]
    weights = 2.0 / (poly_order * node_count * top * top)
    deriv = np.zeros((node_count, node_count))
    for i in range(node_count):
        for j in range(node_count):
            if i != j:
                deriv[i, j] = top[i] / (top[j] * (nodes[i] - nodes[j]))
    deriv[0, 0] = -poly_order * node_count / 4.0
    deriv[poly_order, poly_order] = poly_order * node_count / 4.0
    mass = (weights[:, None, None] * weights[None, :, None] * weights[None, None, :]).reshape(-1)
    line = deriv.T @ (weights[:, None] * deriv)
    scaled = line / weights[None, :]
    eye = np.eye(node_count)
    first = np.kron(scaled, np.eye(64))
    second = np.kron(np.eye(4), np.kron(scaled, eye))
    third = np.kron(np.eye(4), np.kron(eye, scaled))
    diag = np.diag(scaled)
    ones = np.ones(node_count)
    diags = np.stack(
        [
            mass * np.kron(diag, np.kron(ones, ones)),
            mass * np.kron(ones, np.kron(diag, ones)),
            mass * np.kron(ones, np.kron(ones, diag)),
        ]
    )
    hats = np.stack([(1.0 - nodes) / 2.0, (1.0 + nodes) / 2.0])
    coarse = (
        hats[:, None, None, :, None, None]
        * hats[None, :, None, None, :, None]
        * hats[None, None, :, None, None, :]
    ).reshape(8, -1)
    return mass, first, np.concatenate([second, third], axis=1), diags, coarse


def table_pieces(table):
    rest = np.asarray(table, np.float32)
    pieces = []
    for _ in range(PIECES):
        piece = rest.astype(ml_dtypes.bfloat16)
        pieces.append(piece)
        rest = rest - piece.astype(np.float32)
    return np.stack(pieces)


def pieces(value):
    found = []
    for left in reversed(range(PIECES)):
        found.append(value.astype(BF16))
        if left:
            value = value - found[-1].astype(F32)
    return found


def row_mask(slots, height):
    high = lax.shift_right_logical(slots, 7)
    width = slots.shape[1]
    return jnp.broadcast_to(high, (height, width)) == lax.broadcasted_iota(jnp.int32, (height, width), 0)


def lane_hot(slots):
    low = lax.bitwise_and(slots, LO - 1)
    width = slots.shape[1]
    hot = jnp.broadcast_to(low, (LO, width)) == lax.broadcasted_iota(jnp.int32, (LO, width), 0)
    return jnp.where(hot, 1.0, 0.0).astype(BF16)


def spread(values, mask):
    wide = [jnp.where(mask, jnp.broadcast_to(value, mask.shape), 0.0) for value in values]
    return jnp.concatenate([piece for value in wide for piece in pieces(value)], axis=0)


def put(left, hot):
    return lax.dot_general(left, hot, (((1,), (1,)), ((), ())), preferred_element_type=F32)


def table_parts(table):
    return jnp.concatenate(pieces(table), axis=1)


def take(parts, hot, mask):
    found = jnp.dot(parts, jnp.concatenate([hot] * PIECES, axis=0), preferred_element_type=F32)
    return jnp.sum(jnp.where(mask, found, 0.0), axis=0, keepdims=True)


def fold(stacked, height):
    result = stacked[:height]
    for piece in range(1, PIECES):
        result = result + stacked[piece * height : (piece + 1) * height]
    return result


def total(value):
    return jnp.sum(jnp.sum(value, axis=1, keepdims=True), axis=0, keepdims=True)


def place(scalars):
    lane = lax.broadcasted_iota(jnp.int32, (1, LO), 1)
    row = jnp.zeros((1, LO), F32)
    for index, scalar in enumerate(scalars):
        row = jnp.where(lane == index, scalar, row)
    return row


def column(row):
    size = row.shape[1]
    square = lax.broadcasted_iota(jnp.int32, (size, size), 0) == lax.broadcasted_iota(jnp.int32, (size, size), 1)
    return jnp.sum(jnp.where(square, jnp.broadcast_to(row, (size, size)), 0.0), axis=1, keepdims=True)


def flatten(square):
    lane = lax.broadcasted_iota(jnp.int32, (16, ENTRIES), 1)
    sub = lax.broadcasted_iota(jnp.int32, (16, ENTRIES), 0)
    spreader = jnp.where(lax.bitwise_and(lane, 15) == sub, 1.0, 0.0)
    wide = jnp.dot(square, spreader, precision=lax.Precision.HIGHEST, preferred_element_type=F32)
    return jnp.sum(jnp.where(lax.shift_right_logical(lane, 4) == sub, wide, 0.0), axis=0, keepdims=True)


def list_row(split_ref, curve_ref, t):
    return split_ref[0, 0, t : t + 1, :] if t < 2 else curve_ref[0, 0, t - 2 : t - 1, :]


def list_mask(split_ref, curve_ref):
    rows = [list_row(split_ref, curve_ref, t) for t in range(LISTS)]
    return row_mask(jnp.concatenate(rows, axis=1), HI)


def by_list(wide):
    return [wide[:, t * LO : (t + 1) * LO] for t in range(LISTS)]


def point_hot(hot_ref, e):
    return hot_ref[:, e * POINTS : (e + 1) * POINTS]


def owner_mask():
    lane = lax.broadcasted_iota(jnp.int32, (ELEMS, ENTRIES), 1)
    return lax.bitwise_and(lane, 15) == lax.broadcasted_iota(jnp.int32, (ELEMS, ENTRIES), 0)


def coarse_line(scaled, phi_ref, pick_ref):
    acc = jnp.zeros((ELEMS, ENTRIES), F32)
    for v in range(8):
        restricted = jnp.sum(scaled * phi_ref[v : v + 1, :], axis=1, keepdims=True)
        acc = acc + restricted * pick_ref[v]
    return jnp.sum(acc, axis=0, keepdims=True)


def coarse_correction(image, phi_ref, pick_ref, xcols, xhot):
    line = take(table_parts(image), xhot, row_mask(xcols, ROWS))
    result = jnp.zeros((ELEMS, POINTS), F32)
    for v in range(8):
        vertex = jnp.sum(pick_ref[v] * line, axis=1, keepdims=True)
        result = result + vertex * phi_ref[v : v + 1, :]
    return result


def image_of(line, cols, hot):
    return fold(put(spread([line], row_mask(cols, ROWS)), hot), ROWS)


def place_in_curve():
    here = lax.axis_index("curve")
    return lax.div(here, GROUP), lax.rem(here, GROUP)


def kept_row(fits, row):
    return jnp.where(fits, row, jnp.zeros_like(row))


def write_payload(pay_ref, rows_ref, image, rows):
    inner = place_in_curve()[1]
    for g in range(GROUP):
        for r in range(8):
            pay_ref[g, 0:1, r * LO : (r + 1) * LO] = image[8 * g + r : 8 * g + r + 1, :]
        row = jnp.zeros((1, LO), F32)
        for t in range(2, LISTS):
            row = jnp.where(lax.rem(inner + WAYS[t][1] + GROUP, GROUP) == g, rows[t], row)
        pay_ref[g, 0:1, CHUNK:] = row
    rows_ref[...] = jnp.concatenate(rows[:2], axis=0)


def setup_scatter(*refs):
    sources, refs = refs[:15], refs[15:]
    slot_ref, split_ref, curve_ref, mass_ref, phi_ref, first_ref, second_ref = refs[:7]
    hot_ref, sums_ref, scale_ref, entry_ref, pick_ref, xhot_ref = refs[7:13]
    out_refs = refs[13:19]
    rhs_ref, stretch_ref, helm_ref, corner_ref, xvals_ref, xcols_ref, xcount_ref, diag_ref, sems = refs[19:]
    targets = (rhs_ref, stretch_ref, helm_ref, corner_ref, xvals_ref, xcols_ref, xcount_ref, diag_ref) + refs[:7]
    copies = [pltpu.make_async_copy(a, b, sems.at[i]) for i, (a, b) in enumerate(zip(sources, targets))]
    for copy in copies:
        copy.start()
    for copy in copies[:LATE]:
        copy.wait()
    columns = [column(stretch_ref[d : d + 1, :]) for d in range(3)] + [column(helm_ref[...])]
    scale_ref[...] = jnp.concatenate(columns + columns, axis=1)
    diag = columns[3] * mass_ref[...]
    for d in range(3):
        diag = diag + columns[d] * diag_ref[d : d + 1, :]
    live = lax.broadcasted_iota(jnp.int32, (16, 16), 0) < jnp.broadcast_to(xcount_ref[...], (16, 16))
    factor = flatten(jnp.where(live, xvals_ref[...], 0.0))
    cols = flatten(xcols_ref[...].astype(F32))
    entries = (cols + 0.5).astype(jnp.int32)
    entry_ref[...] = entries
    xhot_ref[...] = lane_hot(entries)
    owner = lax.bitwise_and(lax.broadcasted_iota(jnp.int32, (ELEMS, ENTRIES), 1), 15)
    corners = [column(corner_ref[v : v + 1, :].astype(F32)) for v in range(8)]
    for v in range(8):
        pick_ref[v] = jnp.where((corners[v] + 0.5).astype(jnp.int32) == owner, factor, 0.0)
    corner = jnp.concatenate(corners, axis=1)
    lists = jnp.concatenate(
        [column(list_row(split_ref, curve_ref, t).astype(F32)) for t in range(LISTS)], axis=0
    )
    lists = (lists + 0.5).astype(jnp.int32)
    acc = jnp.zeros(((1 + 2 * PIECES) * HI, LO), F32)
    weights = jnp.zeros((PIECES * ELEMS, LISTS * LO), F32)
    for e in range(ELEMS):
        slots = slot_ref[e : e + 1, :]
        hot = lane_hot(slots)
        hot_ref[:, e * POINTS : (e + 1) * POINTS] = hot
        mask = row_mask(slots, HI)
        left = spread([diag[e : e + 1, :], rhs_ref[e : e + 1, :]], mask)
        left = jnp.concatenate([jnp.where(mask, 1.0, 0.0).astype(BF16), left], axis=0)
        acc = acc + put(left, hot)
        unknown = lax.broadcasted_iota(jnp.int32, (ELEMS, 8), 0).astype(F32)
        vertex = jnp.where(jnp.abs(corner[e : e + 1, :] - unknown) < 0.5, 1.0, 0.0)
        basis = jnp.dot(vertex, phi_ref[...], precision=lax.Precision.HIGHEST, preferred_element_type=F32)
        shape = (LISTS * LO, POINTS)
        same = jnp.where(jnp.broadcast_to(slots, shape) == jnp.broadcast_to(lists, shape), 1.0, 0.0)
        weights = weights + put(jnp.concatenate(pieces(basis), axis=0), same.astype(BF16))
    weights = fold(weights, ELEMS)
    tables = []
    for field in range(3):
        first = HI + PIECES * HI * (field - 1)
        table = fold(acc[first : first + PIECES * HI], HI) if field else acc[:HI]
        sums_ref[field] = table
        tables.append(table_parts(table))
    slots = jnp.concatenate([list_row(split_ref, curve_ref, t) for t in range(LISTS)], axis=1)
    hot = lane_hot(slots)
    hot_ref[:, WIDE:] = hot
    mask = row_mask(slots, HI)
    rows = [take(tables[field], hot, mask) for field in range(3)]
    plain = [cols[:, :LO], cols[:, LO:], factor[:, :LO], factor[:, LO:], jnp.zeros((1, LO), F32)]
    for t in range(LISTS):
        lanes = slice(t * LO, (t + 1) * LO)
        out_refs[t][...] = jnp.concatenate([row[:, lanes] for row in rows] + plain + [weights[:, lanes]], axis=0)
    for copy in copies[LATE:]:
        copy.wait()


def incoming_table(split_ref, curve_ref, hot_ref, rows):
    left = spread([jnp.concatenate(rows, axis=1)], list_mask(split_ref, curve_ref))
    return fold(put(left, hot_ref[:, WIDE:]), HI)


def setup_gather(slot_ref, split_ref, curve_ref, hot_ref, sums_ref, phi_ref, pick_ref, entry_ref, xhot_ref, *refs):
    blocks = refs[:LISTS]
    minv_ref, dinv_ref, right_ref, nline_ref, nentry_ref, nhot_ref, weight_ref, pay_ref, rows_ref = refs[LISTS:]
    tables = [
        table_parts(
            sums_ref[field] + incoming_table(split_ref, curve_ref, hot_ref, [block[field : field + 1, :] for block in blocks])
        )
        for field in range(3)
    ]
    for e in range(ELEMS):
        mask = row_mask(slot_ref[e : e + 1, :], HI)
        hot = point_hot(hot_ref, e)
        minv_ref[e : e + 1, :] = 1.0 / take(tables[0], hot, mask)
        dinv_ref[e : e + 1, :] = 1.0 / take(tables[1], hot, mask)
        right_ref[e : e + 1, :] = take(tables[2], hot, mask)
    mult = take(tables[0], hot_ref[:, WIDE:], list_mask(split_ref, curve_ref))
    rows = by_list(jnp.where(mult > 0.5, 1.0 / jnp.where(mult > 0.5, mult, 1.0), 0.0))
    own = entry_ref[...]
    nentry_ref[:, :ENTRIES] = own
    nhot_ref[:, :ENTRIES] = xhot_ref[...]
    for t in range(LISTS):
        there = jnp.concatenate([blocks[t][3:4, :], blocks[t][4:5, :]], axis=1)
        weight_ref[t] = blocks[t][8:24, :]
        entries = (there + 0.5).astype(jnp.int32)
        lanes = slice((t + 1) * ENTRIES, (t + 2) * ENTRIES)
        nentry_ref[:, lanes] = entries
        nhot_ref[:, lanes] = lane_hot(entries)
        nline_ref[t : t + 1, :] = jnp.concatenate([blocks[t][5:6, :], blocks[t][6:7, :]], axis=1)
    line = coarse_line(right_ref[...] * minv_ref[...], phi_ref, pick_ref)
    write_payload(pay_ref, rows_ref, image_of(line, entry_ref[...], xhot_ref[...]), rows)


def operator(u, scale_ref, mass_ref, first_ref, second_ref):
    def product(parts, ref):
        rows = parts[0].shape[0]
        one = jnp.dot(jnp.concatenate(parts, axis=0), ref[0], preferred_element_type=F32)
        two = jnp.dot(jnp.concatenate(parts[:2], axis=0), ref[1], preferred_element_type=F32)
        three = jnp.dot(parts[0], ref[2], preferred_element_type=F32)
        return one[:rows] + (one[rows : 2 * rows] + two[:rows] + (one[2 * rows :] + two[rows:] + three))

    half = POINTS // 2
    parts = pieces(u)
    along = product(parts, first_ref)
    inside = product([jnp.concatenate([p[:, :half], p[:, half:]], axis=0) for p in parts], second_ref)
    second = jnp.concatenate([inside[:ELEMS, :half], inside[ELEMS:, :half]], axis=1)
    third = jnp.concatenate([inside[:ELEMS, half:], inside[ELEMS:, half:]], axis=1)
    result = scale_ref[:, 0:1] * along + scale_ref[:, 1:2] * second + scale_ref[:, 2:3] * third
    return mass_ref[...] * (result + scale_ref[:, 3:4] * u)


def scatter_points(field_ref, slot_ref, hot_ref):
    acc = jnp.zeros((PIECES * HI, LO), F32)
    for e in range(ELEMS):
        left = spread([field_ref[e : e + 1, :]], row_mask(slot_ref[e : e + 1, :], HI))
        acc = acc + put(left, point_hot(hot_ref, e))
    return fold(acc, HI)


def gather_points(table, slot_ref, hot_ref, out_ref):
    parts = table_parts(table)
    for e in range(ELEMS):
        out_ref[e : e + 1, :] = take(parts, point_hot(hot_ref, e), row_mask(slot_ref[e : e + 1, :], HI))


def send_lists(table, split_ref, curve_ref, hot_ref):
    return by_list(take(table_parts(table), hot_ref[:, WIDE:], list_mask(split_ref, curve_ref)))


def coarse_shift(image, earlier):
    factors = []
    for other in earlier:
        size = total(other * other)
        fits = size > 1e-30
        factors.append(jnp.where(fits, total(image * other) / jnp.where(fits, size, 1.0), 0.0))
    for factor, other in zip(factors, earlier):
        image = image - factor * other
    return factors, image


def krylov_step(index, last, *refs):
    (slot_ref, split_ref, curve_ref, hot_ref, scale_ref, mass_ref, first_ref, second_ref, phi_ref, pick_ref,
     entry_ref, xhot_ref, nline_ref, nentry_ref, nhot_ref, minv_ref, dinv_ref, norm_ref, gathered_ref,
     halo_ref) = refs[:20]
    refs = refs[20:]
    image_ref, field_ref = refs[-2:]
    refs = refs[:-2]
    rows = [halo_ref[t : t + 1, :] for t in range(LISTS)]
    if index == 0:
        right_ref, plain_ref = refs[:2]
        refs = refs[2:]
        force = right_ref[...]
    else:
        weight_ref, sums_ref = refs[:2]
        refs = refs[2:]
        olds, refs = refs[: 2 * index], refs[2 * index :]
        base_refs, coarse_refs = olds[:index], olds[index:]
    base_ref, newnorm_ref, newsums_ref = refs[:3]
    refs = refs[3:]
    if index == 0:
        newweight_ref = refs[0]
        refs = refs[1:]
        for t in range(LISTS):
            newweight_ref[t] = plain_ref[t] * rows[t]
        weight_ref = newweight_ref
    else:
        force_ref = refs[0]
        refs = refs[1:]
        gather_points(
            sums_ref[...] + incoming_table(split_ref, curve_ref, hot_ref, rows), slot_ref, hot_ref, force_ref
        )
        force = force_ref[...]
    for g in range(GROUP):
        for r in range(8):
            image_ref[8 * g + r : 8 * g + r + 1, :] = gathered_ref[g, 0:1, r * LO : (r + 1) * LO]
    image = image_ref[...]
    correction = coarse_correction(image, phi_ref, pick_ref, entry_ref[...], xhot_ref[...])
    base = force * dinv_ref[...] + correction
    if index:
        factors, image = coarse_shift(image, [ref[...] for ref in coarse_refs])
        for factor, ref in zip(factors, base_refs):
            base = base - factor * ref[...]
    else:
        factors = []
    size = 1.0 + jnp.sqrt(total(image * image))
    base = base * (1.0 / size)
    base_ref[...] = base
    if not last:
        coarse_ref, *refs = refs
        coarse_ref[...] = image * (1.0 / size)
    newnorm_ref[...] = norm_ref[...]
    newnorm_ref[index : index + 1, :] = place(factors + [size])
    field_ref[...] = operator(base, scale_ref, mass_ref, first_ref, second_ref)
    table = scatter_points(field_ref, slot_ref, hot_ref)
    newsums_ref[...] = table
    rows = send_lists(table, split_ref, curve_ref, hot_ref)
    if last:
        for t in range(LISTS):
            refs[t][...] = rows[t]
        return
    pay_ref, rows_ref = refs
    gather_points(table, slot_ref, hot_ref, field_ref)
    line = coarse_line(field_ref[...] * minv_ref[...], phi_ref, pick_ref)
    lines = [line]
    owner = owner_mask()
    for t in range(LISTS):
        loads = jnp.sum(weight_ref[t] * rows[t], axis=1, keepdims=True)
        lines.append(jnp.sum(jnp.where(owner, loads, 0.0), axis=0, keepdims=True) * nline_ref[t : t + 1, :])
    image = image_of(jnp.concatenate(lines, axis=1), nentry_ref[...], nhot_ref[...])
    write_payload(pay_ref, rows_ref, image, rows)


def sum_chunk(got_ref):
    chunk = got_ref[0, 0:1, :CHUNK]
    for g in range(1, GROUP):
        chunk = chunk + got_ref[g, 0:1, :CHUNK]
    return chunk


def after_inner(got_ref, rows_ref, pay_ref, chalo_ref):
    inner = place_in_curve()[1]
    for t in range(2, LISTS):
        there = lax.rem(inner + WAYS[t][1] + GROUP, GROUP)
        chalo_ref[t - 2 : t - 1, :] = got_ref[there, 0:1, CHUNK:]
    chunk = sum_chunk(got_ref)
    here = lax.axis_index("split")
    for g in range(GROUP):
        pay_ref[g, 0:1, :CHUNK] = chunk
        row = jnp.where(here - 1 == g, rows_ref[0:1, :], kept_row(here + 1 == g, rows_ref[1:2, :]))
        pay_ref[g, 0:1, CHUNK:] = row


def after_split(got_ref, chalo_ref, pay_ref, shalo_ref):
    here = lax.axis_index("split")
    for t in range(2):
        there = here + WAYS[t][1]
        row = got_ref[jnp.clip(there, 0, GROUP - 1), 0:1, CHUNK:]
        shalo_ref[t : t + 1, :] = kept_row(jnp.logical_and(there >= 0, there < GROUP), row)
    chunk = sum_chunk(got_ref)
    outer = place_in_curve()[0]
    up = jnp.concatenate([chalo_ref[1:2, :], chalo_ref[0:1, :]], axis=1)
    down = jnp.concatenate([chalo_ref[2:3, :], chalo_ref[3:4, :]], axis=1)
    for g in range(GROUP):
        pay_ref[g, 0:1, :CHUNK] = chunk
        pay_ref[g, 0:1, CHUNK:] = jnp.where(outer + 1 == g, up, kept_row(outer - 1 == g, down))


def after_outer(got_ref, shalo_ref, chalo_ref, pay_ref, halo_ref):
    chunk = sum_chunk(got_ref)
    for g in range(GROUP):
        pay_ref[g] = chunk
    outer, inner = place_in_curve()
    rows = [shalo_ref[t : t + 1, :] for t in range(2)]
    for t in range(2, LISTS):
        offset = WAYS[t][1]
        beyond = inner + offset >= GROUP if offset > 0 else inner + offset < 0
        there = outer + (1 if offset > 0 else -1)
        lane = CHUNK + (abs(offset) - 1) * LO
        far = got_ref[jnp.clip(there, 0, GROUP - 1), 0:1, lane : lane + LO]
        far = kept_row(jnp.logical_and(there >= 0, there < GROUP), far)
        rows.append(jnp.where(beyond, far, chalo_ref[t - 2 : t - 1, :]))
    halo_ref[...] = jnp.concatenate(rows, axis=0)


def gram(*refs):
    slot_ref, split_ref, curve_ref, hot_ref, sums_ref, minv_ref, right_ref = refs[:7]
    base_refs, force_refs = refs[7:11], refs[11:14]
    last_ref, pay_ref = refs[20:]
    rows = [ref[...] for ref in refs[14:20]]
    gather_points(
        sums_ref[...] + incoming_table(split_ref, curve_ref, hot_ref, rows), slot_ref, hot_ref, last_ref
    )
    weighted = [ref[...] * minv_ref[...] for ref in base_refs]
    scalars = []
    for ref in (right_ref, *force_refs, last_ref):
        scalars += [total(ref[...] * base) for base in weighted]
    row = place(scalars)
    for g in range(pay_ref.shape[0]):
        pay_ref[g] = row


def finish(*refs):
    got_ref, norm_ref, right_ref = refs[:3]
    base_refs, force_refs = refs[3:7], refs[7:11]
    solution_ref, residual_ref = refs[11:]
    sums = [got_ref[g] for g in range(8)]
    for g in range(8, got_ref.shape[0]):
        sums[g % 8] = sums[g % 8] + got_ref[g]
    row = ((sums[0] + sums[1]) + (sums[2] + sums[3])) + ((sums[4] + sums[5]) + (sums[6] + sums[7]))
    table = [[row[:, 4 * i + j : 4 * i + j + 1] for j in range(4)] for i in range(5)]
    relation = [[norm_ref[i : i + 1, j : j + 1] for j in range(i + 1)] for i in range(4)]

    def pair(left, right):
        acc = None
        for i, a in enumerate(left):
            inner = None
            for j, b in enumerate(right):
                if b is not None:
                    inner = b * table[i][j] if inner is None else inner + b * table[i][j]
            if a is not None and inner is not None:
                acc = a * inner if acc is None else acc + a * inner
        return acc

    def less(value, factor, other):
        if other is None:
            return value
        return -factor * other if value is None else value - factor * other

    residual = [jnp.ones((1, 1), F32)] + [None] * 4
    precond = [relation[0][0]] + [None] * 3
    direction = list(precond)
    solution = [None] * 4
    rz = pair(residual, precond)
    for k in range(ITERS):
        moved = [None] + direction
        alpha = rz / pair(moved, direction)
        solution = [less(value, -alpha, other) for value, other in zip(solution, direction)]
        residual = [less(value, alpha, other) for value, other in zip(residual, moved)]
        if k < ITERS - 1:
            shifted = [None] * 4
            for j, d in enumerate(direction[:3]):
                if d is not None:
                    for i, factor in enumerate(relation[j + 1]):
                        shifted[i] = less(shifted[i], -d, factor)
            precond = [less(value, alpha, other) for value, other in zip(precond, shifted)]
            rz_next = pair(residual, precond)
            beta = rz_next / rz
            direction = [less(value, -beta, other) for value, other in zip(precond, direction)]
            rz = rz_next
    result = solution[0] * base_refs[0][...]
    for j in range(1, 4):
        result = result + solution[j] * base_refs[j][...]
    solution_ref[...] = result
    result = right_ref[...]
    for j in range(4):
        result = result + residual[j + 1] * force_refs[j][...]
    residual_ref[...] = result


def run(body, name, args, outs, scratch=(), where=pltpu.VMEM):
    return pl.pallas_call(
        body,
        name=name,
        out_shape=[jax.ShapeDtypeStruct(shape, dtype) for shape, dtype in outs],
        in_specs=[pl.BlockSpec(memory_space=where) for _ in args],
        out_specs=[pl.BlockSpec(memory_space=pltpu.VMEM) for _ in outs],
        scratch_shapes=list(scratch),
        compiler_params=pltpu.CompilerParams(vmem_limit_bytes=VMEM_LIMIT),
    )(*args)


def shift(block, axis, offset):
    size = lax.axis_size(axis)
    route = [(i, i + offset) for i in range(size) if 0 <= i + offset < size]
    return lax.ppermute(block, axis, route)


WAYS = (("split", -1), ("split", 1), ("curve", -2), ("curve", -1), ("curve", 1), ("curve", 2))


def exchange(outgoing):
    arrived = [None] * LISTS
    for t, (axis, offset) in enumerate(WAYS):
        back = WAYS.index((axis, -offset))
        arrived[back] = shift(outgoing[t], axis, offset)
    return arrived


def reduce_image(pay, rows):
    size = lax.axis_size("curve")
    near = [list(range(first, first + GROUP)) for first in range(0, size, GROUP)]
    far = [list(range(first, size, GROUP)) for first in range(GROUP)]

    def frame(count):
        return ((GROUP, 1, CHUNK + count * LO), F32)

    got = lax.all_to_all(pay, "curve", 0, 0, axis_index_groups=near)
    pay, chalo = run(after_inner, "after_inner", (got, rows), [frame(1), ((4, LO), F32)])
    got = lax.all_to_all(pay, "split", 0, 0)
    pay, shalo = run(after_split, "after_split", (got, chalo), [frame(2), ((2, LO), F32)])
    got = lax.all_to_all(pay, "curve", 0, 0, axis_index_groups=far)
    pay, halo = run(after_outer, "after_outer", (got, shalo, chalo), [frame(0), ((LISTS, LO), F32)])
    return lax.all_to_all(pay, "curve", 0, 0, axis_index_groups=near), halo


def local(rhs_load, stretch, helm_shift, local_slot, share_curve, share_split, coarse_slot, x_vals, x_cols, x_count):
    mass, first, second, diags, coarse = element_tables()
    mass = jnp.asarray(mass.reshape(1, -1), F32)
    diags = jnp.asarray(diags, F32)
    phi = jnp.asarray(coarse, F32)
    first = jnp.asarray(table_pieces(first))
    second = jnp.asarray(table_pieces(second))
    field = ((ELEMS, POINTS), F32)
    table = ((HI, LO), F32)
    line = ((1, LO), F32)
    payload = [((GROUP, 1, CHUNK + LO), F32), ((2, LO), F32)]
    sent = [((24, LO), F32)] * LISTS
    sent_last = [line] * LISTS
    entry = jnp.int32

    sources = (rhs_load, stretch, helm_shift.reshape(1, -1), coarse_slot, x_vals, x_cols, x_count.reshape(1, -1), diags,
               local_slot, share_split, share_curve, mass, phi, first, second)
    kept = [(array.shape, array.dtype) for array in sources[8:]]
    outs = kept + [
        ((LO, WIDE + LISTS * LO), BF16), ((3, HI, LO), F32), ((ELEMS, 8), F32), ((1, ENTRIES), entry),
        ((8, ELEMS, ENTRIES), F32), ((LO, ENTRIES), BF16),
    ] + sent
    scratch = [pltpu.VMEM(array.shape, array.dtype) for array in sources[:8]]
    scratch.append(pltpu.SemaphoreType.DMA((len(sources),)))
    (local_slot, share_split, share_curve, mass, phi, first, second, hot, sums3, scale, entries, pick, xhot,
     *outgoing) = run(setup_scatter, "setup_scatter", tuple(pltpu.with_memory_space_constraint(a, pltpu.HBM) for a in sources), outs, scratch, pltpu.HBM)
    arrived = exchange(outgoing)
    shape = (local_slot, share_split, share_curve, hot)
    minv, dinv, right, nline, nentry, nhot, plain, pay, rows = run(
        setup_gather,
        "setup_gather",
        (*shape, sums3, phi, pick, entries, xhot, *arrived),
        [field, field, field, ((LISTS, ENTRIES), F32), ((1, (LISTS + 1) * ENTRIES), entry), ((LO, (LISTS + 1) * ENTRIES), BF16),
         ((LISTS, ELEMS, LO), F32)]
        + payload,
    )
    common = (*shape, scale, mass, first, second, phi, pick, entries, xhot, nline, nentry, nhot, minv, dinv)
    scratch = [pltpu.VMEM((ROWS, LO), F32), pltpu.VMEM((ELEMS, POINTS), F32)]
    norm = jnp.ones((8, LO), F32)
    bases, forces, coarses = [], [], []
    for index in range(ITERS):
        last = index == ITERS - 1
        gathered, halo = reduce_image(pay, rows)
        own = (right, plain) if index == 0 else (weight, sums, *bases, *coarses)
        outs = [field, ((8, LO), F32), table] + [((LISTS, ELEMS, LO), F32) if index == 0 else field]
        outs += [] if last else [((ROWS, LO), F32)]
        base, norm, sums, extra, *rest = run(
            functools.partial(krylov_step, index, last),
            f"krylov_step{index}",
            (*common, norm, gathered, halo, *own),
            outs + (sent_last if last else payload),
            scratch,
        )
        bases.append(base)
        if index == 0:
            weight = extra
        else:
            forces.append(extra)
        if not last:
            coarse, pay, rows = rest
            coarses.append(coarse)
    devices = lax.axis_size("curve") * lax.axis_size("split")
    force, pay = run(
        gram,
        "gram",
        (*shape, sums, minv, right, *bases, *forces, *exchange(rest)),
        [field, ((devices, 1, LO), F32)],
    )
    got = lax.all_to_all(pay, ("curve", "split"), 0, 0)
    solution, residual = run(
        finish, "finish", (got, norm, right, *bases, *forces, force), [field, field]
    )
    return solution, residual


def solution(mesh):
    in_specs = (
        P(("curve", "split"), None),
        P(None, ("curve", "split")),
        P(("curve", "split")),
        P(("curve", "split"), None),
        P("curve", "split", None, None),
        P("curve", "split", None, None),
        P(None, ("curve", "split")),
        P(None, ("curve", "split")),
        P(None, ("curve", "split")),
        P(("curve", "split")),
    )
    out_specs = (P(("curve", "split"), None), P(("curve", "split"), None))
    return jax.shard_map(local, mesh=mesh, in_specs=in_specs, out_specs=out_specs, check_vma=False)
```
